256 devices in a mesh: ctx: 32 (over y, x, core), seq: 8 (over z).
Axes of the slice: x: 4, y: 4, z: 8, core: 2. Of those that a mesh axis runs over, the one named last changes fastest.
Arguments:
- queries: bfloat16 [32768, 4096], P(('seq', 'ctx')), may hold values from -6 to 6
- key_proj: bfloat16 [32768, 4096], P(('seq', 'ctx')), may hold values from -6 to 6
- value_proj: bfloat16 [32768, 4096], P(('seq', 'ctx')), may hold values from -6 to 6
- decay_rate: float32 [16, 4096], P(None, 'ctx'), may hold values from 3.0517578e-06 to 0.06
- residue: float32 [16, 4096], P(None, 'ctx'), may hold values from -1 to 1
- skip_gain: float32 [4096], P('ctx'), may hold values from -1 to 1
Outputs:
- operator_out: bfloat16 [32768, 4096], P(('seq', 'ctx'))
The draws below stay inside these ranges and needn't reach their ends.
All inputs are finite; a program needn't handle non-finite values.
Results may differ from the reference program's by a relative error of at most 0.011.
Values may be sent and summed in bfloat16 or wider, within the bound.
No kernel may reach another device: no remote copies, remote signals or barrier semaphores. Data moves between devices by JAX's collectives and lax.ppermute only.
A program may use at most 320 MiB of HBM per device.

```python
import math
import jax
import jax.numpy as jnp
from jax import lax

D = 4096
MODES = 16
LENGTH = 32768
N_CTX = 32


def draw_decay_rate(key, part):
    pick_key, slow_key, fast_key = jax.random.split(key, 3)
    shape = (MODES, D)
    slow_low = math.log(0.1 / LENGTH)
    slow_high = math.log(2.3 / LENGTH)
    fast_high = math.log(0.06)
    share = 0.5
    slow_rates = jnp.exp(jax.random.uniform(slow_key, shape, jnp.float32, slow_low, slow_high))
    fast_rates = jnp.exp(jax.random.uniform(fast_key, shape, jnp.float32, slow_high, fast_high))
    chosen = jax.random.uniform(pick_key, shape, jnp.float32) < share
    return jnp.where(chosen, slow_rates, fast_rates).astype(jnp.float32)


def steps_of(key, shape, cuts, smallest, top_value):
    factor_of, own = 1.0, jax.random.fold_in(key, 6)
    for dim, parts in cuts:
        steps = jnp.exp(jax.random.uniform(jax.random.fold_in(own, dim), (parts,), jnp.float32, smallest / len(cuts), top_value / len(cuts)))
        factor_of = factor_of * jnp.repeat(steps, shape[dim] // parts).reshape([-1 if axis == dim else 1 for axis in range(len(shape))])
    return factor_of


def bell_draw(key, shape, width, reach, cuts=(), held_as=jnp.bfloat16):
    loudness = steps_of(key, shape, cuts, -0.22, 0.18) if cuts else 1.0
    entries = jax.random.normal(key, shape, jnp.float32) * width * loudness
    return jnp.minimum(jnp.maximum(entries, -reach), reach).astype(held_as)


def setup_inputs(seed: int = 0) -> dict:
    streams_of = jax.random.split(jax.random.key(seed), 7)
    return {
        "queries": bell_draw(streams_of[0], (LENGTH, D), 1.0, 6.0, ((0, 256),)),
        "key_proj": bell_draw(streams_of[1], (LENGTH, D), 1.0, 6.0, ((0, 256),)),
        "value_proj": bell_draw(streams_of[2], (LENGTH, D), 1.0, 6.0, ((0, 256),)),
        "decay_rate": draw_decay_rate(jax.random.fold_in(streams_of[6], 71), 0),
        "residue": bell_draw(streams_of[4], (MODES, D), 0.25, 1.0, ((1, 32),), jnp.float32),
        "skip_gain": jnp.clip(jax.random.uniform(streams_of[5], (D,), jnp.float32, -1.0, 1.0) * steps_of(streams_of[5], (D,), ((0, 32),), -0.4, 0.0), -1.0, 1.0),
    }


def link_states(earlier, later):
    return (later[1] * earlier[0] + later[0], earlier[1] * later[1])

def mode_tables(rate, resid, block_len):
    lag_steps = jnp.arange(block_len, dtype=jnp.float32)
    powers = jnp.exp(-rate[None, :, :] * lag_steps[:, None, None])
    weight = resid * jnp.sqrt(-jnp.expm1(-2.0 * rate))
    return (powers, weight)

def local_pass(signal, powers, weight, rate, block_len):
    length, columns = signal.shape
    nblocks = length // block_len
    kernel = jnp.einsum('jmc,mc->jc', powers, weight, precision=lax.Precision.HIGHEST)
    lag_grid = jnp.arange(block_len, dtype=jnp.int32)[:, None] - jnp.arange(block_len, dtype=jnp.int32)[None, :]
    toeplitz = jnp.where((lag_grid >= 0)[:, :, None], kernel[jnp.clip(lag_grid, 0, block_len - 1)], 0.0)
    blocks = signal.reshape(nblocks, block_len, columns)
    inner_part = jnp.einsum('tsc,bsc->btc', toeplitz, blocks, precision=lax.Precision.HIGHEST)
    block_ends = jnp.einsum('bsc,smc->bmc', blocks, powers[::-1], precision=lax.Precision.HIGHEST)
    block_decay = jnp.broadcast_to(jnp.exp(-rate * block_len)[None], block_ends.shape)
    run_states, run_decay = lax.associative_scan(link_states, (block_ends, block_decay), axis=0)
    before = jnp.concatenate([jnp.zeros_like(run_states[:1]), run_states[:-1]], axis=0)
    return (inner_part, before, run_states[-1])

def finish(inner_part, before, start_state, powers, weight, rate, block_len):
    nblocks = before.shape[0]
    block_starts = jnp.arange(nblocks, dtype=jnp.float32) * block_len
    offsets = jnp.exp(-rate[None, :, :] * block_starts[:, None, None])
    states = before + offsets * start_state[None]
    lift_table = powers * (jnp.exp(-rate) * weight)[None]
    carried = jnp.einsum('bmc,tmc->btc', states, lift_table, precision=lax.Precision.HIGHEST)
    return (inner_part + carried).reshape(nblocks * block_len, -1)

def reference(queries, key_proj, value_proj, decay_rate, residue, skip_gain):
    mixed_rows = (key_proj.astype(jnp.float32) * value_proj.astype(jnp.float32)).astype(jnp.bfloat16)
    length = queries.shape[0]
    columns = queries.shape[1]
    groups = N_CTX
    group_width = columns // groups
    block_len = math.gcd(length, 32)

    def split_cols(array):
        return array.reshape(array.shape[0], groups, group_width).transpose(1, 0, 2)

    def one_group(pieces):
        query_g, mixed_g, rate_g, resid_g, gain_g = pieces
        signal = mixed_g.astype(jnp.float32)
        powers, weight = mode_tables(rate_g, resid_g, block_len)
        inner_part, before, end_state = local_pass(signal, powers, weight, rate_g, block_len)
        filtered = finish(inner_part, before, jnp.zeros_like(end_state), powers, weight, rate_g, block_len)
        pre_gate = lax.optimization_barrier((filtered + gain_g[None, :] * signal).astype(jnp.bfloat16))
        return (query_g.astype(jnp.float32) * pre_gate.astype(jnp.float32)).astype(jnp.bfloat16)
    results = lax.map(one_group, (split_cols(queries), split_cols(mixed_rows), split_cols(decay_rate), split_cols(residue), skip_gain.reshape(groups, group_width)))
    return results.transpose(1, 0, 2).reshape(length, columns)
```

```python
import functools

import jax
import jax.numpy as jnp
from jax import lax
from jax.experimental import pallas as pl
from jax.experimental.pallas import tpu as pltpu
from jax.sharding import PartitionSpec as P

F32, BF16 = jnp.float32, jnp.bfloat16
LANES = 128
SUB = 8
CHUNK = 128
SEGS = 8
STEPS = CHUNK // SEGS
MODES = 16
ROWS = CHUNK + 4 * MODES


def one_minus_exp(x):
    series = jnp.ones_like(x)
    for order in range(9, 1, -1):
        series = 1.0 - x * (1.0 / order) * series
    return jnp.where(x < 0.5, x * series, 1.0 - jnp.exp(-x))


def pack_kernel(k_ref, v_ref, rate_ref, resid_ref, gain_ref, out_ref, par, taps):
    @pl.when(pl.program_id(0) == 0)
    def _():
        rate = rate_ref[...]
        weight = resid_ref[...] * jnp.sqrt(one_minus_exp(2.0 * rate))
        power = jnp.exp(-rate)
        high = rate.astype(BF16)
        term = weight
        for lag in range(STEPS):
            tap = jnp.sum(term, axis=0, keepdims=True)
            taps[lag : lag + 1, :] = tap + gain_ref[...] if lag == 0 else tap
            term = term * power
        par[0:16, :] = high
        par[16:32, :] = (rate - high.astype(F32)).astype(BF16)
        par[32:48, :] = weight.astype(BF16)
        par[48:64, :] = taps[...].astype(BF16)

    for g in range(out_ref.shape[0]):
        cols = slice(g * LANES, (g + 1) * LANES)
        out_ref[g, 0:CHUNK, :] = (k_ref[:, cols].astype(F32) * v_ref[:, cols].astype(F32)).astype(BF16)
        out_ref[g, CHUNK:ROWS, :] = par[...]


def states_kernel(in_ref, rate_ref, before_ref, end_ref, sig, ends):
    step = pl.program_id(0)
    nchunks = before_ref.shape[0]
    for i in range(SUB):
        sig[i * CHUNK : (i + 1) * CHUNK, :] = in_ref[i].astype(F32)
    power = jnp.exp(-rate_ref[...])
    powers = [jnp.broadcast_to(power[m : m + 1, :], (SUB, LANES)) for m in range(MODES)]

    def token(t, states):
        x = sig[pl.ds(t, SUB, stride=CHUNK), :]
        return tuple(powers[m] * states[m] + x for m in range(MODES))

    zero = jnp.zeros((SUB, LANES), F32)
    states = lax.fori_loop(0, CHUNK, token, (zero,) * MODES, unroll=8)
    for m in range(MODES):
        ends[pl.ds(pl.multiple_of(m * nchunks + step * SUB, SUB), SUB), :] = states[m]

    @pl.when(step == pl.num_programs(0) - 1)
    def _():
        decay = jnp.exp(-float(CHUNK) * rate_ref[...])
        state = jnp.zeros((MODES, LANES), F32)
        for d in range(nchunks):
            before_ref[d] = state
            state = decay * state + ends[pl.ds(d, MODES, stride=nchunks), :]
        end_ref[...] = state


def inner_kernel(send_ref, par_ref, after_ref, y_ref, seg_ref, sig, ends):
    def group(g, carry):
        sig[...] = send_ref[g].astype(F32)
        rate = par_ref[g, 0:16, :].astype(F32) + par_ref[g, 16:32, :].astype(F32)
        weight = par_ref[g, 32:48, :].astype(F32)
        taps = par_ref[g, 48:64, :].astype(F32)
        power = jnp.exp(-rate)
        xs = [sig[pl.ds(t, SEGS, stride=STEPS), :] for t in range(STEPS)]
        tap = [jnp.broadcast_to(taps[j : j + 1, :], (SEGS, LANES)) for j in range(STEPS)]
        for t in range(STEPS):
            acc = tap[0] * xs[t]
            for j in range(1, t + 1):
                acc = acc + tap[j] * xs[t - j]
            y_ref[g, t] = acc
        for m in range(MODES):
            a = jnp.broadcast_to(power[m : m + 1, :], (SEGS, LANES))
            state = xs[0]
            for t in range(1, STEPS):
                state = a * state + xs[t]
            ends[m * SEGS : (m + 1) * SEGS, :] = state
        decay = jnp.exp(-float(STEPS) * rate)
        lift = weight * power
        state = jnp.zeros((MODES, LANES), F32)
        for i in range(SEGS):
            seg_ref[g, i] = lift * state
            state = decay * state + ends[pl.ds(i, MODES, stride=SEGS), :]
        return carry

    lax.fori_loop(0, send_ref.shape[0], group, 0)


def link_kernel(place_ref, before_ref, blocks_ref, rate_ref, out_ref):
    nchunks = before_ref.shape[0]
    place = place_ref[0]
    span = jnp.exp(-float(CHUNK * nchunks) * rate_ref[...])
    start = jnp.zeros((MODES, LANES), F32)
    for z in range(blocks_ref.shape[0]):
        start = jnp.where(z < place, span * start + blocks_ref[z], start)
    decay = jnp.exp(-float(CHUNK) * rate_ref[...])
    for d in range(nchunks):
        out_ref[d] = (before_ref[d] + start).astype(BF16)
        start = decay * start


def final_kernel(start_ref, par_ref, y_ref, seg_ref, q_ref, out_ref, segs, pre):
    for g in range(y_ref.shape[0]):
        rate = par_ref[g, 0:16, :].astype(F32) + par_ref[g, 16:32, :].astype(F32)
        weight = par_ref[g, 32:48, :].astype(F32)
        power = jnp.exp(-rate)
        decay = jnp.exp(-float(STEPS) * rate)
        lifted = weight * power * start_ref[g].astype(F32)
        for i in range(SEGS):
            segs[pl.ds(i, MODES, stride=SEGS), :] = seg_ref[g, i] + lifted
            lifted = lifted * decay
        terms = [segs[m * SEGS : (m + 1) * SEGS, :] for m in range(MODES)]
        powers = [jnp.broadcast_to(power[m : m + 1, :], (SEGS, LANES)) for m in range(MODES)]
        for t in range(STEPS):
            layer = list(terms)
            while len(layer) > 1:
                layer = [layer[i] + layer[i + 1] for i in range(0, len(layer), 2)]
            pre[pl.ds(t, SEGS, stride=STEPS), :] = y_ref[g, t] + layer[0]
            if t < STEPS - 1:
                terms = [terms[m] * powers[m] for m in range(MODES)]
        cols = slice(g * LANES, (g + 1) * LANES)
        gate = pre[...].astype(BF16).astype(F32)
        out_ref[:, cols] = (q_ref[:, cols].astype(F32) * gate).astype(BF16)


def cost(flops, nbytes):
    return pl.CostEstimate(flops=flops, bytes_accessed=nbytes, transcendentals=0)


def local(queries, key_proj, value_proj, decay_rate, residue, skip_gain, *, interpret=False):
    tokens, channels = queries.shape
    groups = channels // LANES
    per = 8
    grid = groups // per
    full = pl.BlockSpec((MODES, LANES), lambda i: (0, 0))
    wide = pl.BlockSpec((CHUNK, per * LANES), lambda i: (0, i))
    state4 = jax.ShapeDtypeStruct((groups, MODES, LANES), F32)

    send = pl.pallas_call(
        pack_kernel,
        grid=(grid,),
        in_specs=[wide, wide, full, full, pl.BlockSpec((1, LANES), lambda i: (0, 0))],
        out_specs=pl.BlockSpec((per, ROWS, LANES), lambda i: (i, 0, 0)),
        out_shape=jax.ShapeDtypeStruct((groups, ROWS, LANES), BF16),
        scratch_shapes=[pltpu.VMEM((4 * MODES, LANES), BF16), pltpu.VMEM((STEPS, LANES), F32)],
        cost_estimate=cost(1_000_000, 4_000_000),
        interpret=interpret,
        name="pack",
    )(key_proj, value_proj, decay_rate, residue, skip_gain[None, :])

    got = lax.all_to_all(send, "ctx", split_axis=0, concat_axis=0, tiled=True)

    before, end_state = pl.pallas_call(
        states_kernel,
        grid=(groups // SUB,),
        in_specs=[pl.BlockSpec((SUB, CHUNK, LANES), lambda i: (i, 0, 0)), full],
        out_specs=[pl.BlockSpec((groups, MODES, LANES), lambda i: (0, 0, 0)), full],
        out_shape=[state4, jax.ShapeDtypeStruct((MODES, LANES), F32)],
        scratch_shapes=[
            pltpu.VMEM((SUB * CHUNK, LANES), F32),
            pltpu.VMEM((MODES * groups, LANES), F32),
        ],
        cost_estimate=cost(20_000_000, 1_300_000),
        interpret=interpret,
        name="states",
    )(got, decay_rate)

    nseq = lax.axis_size("seq")
    blocks = lax.all_to_all(
        jnp.broadcast_to(end_state[None], (nseq, MODES, LANES)),
        "seq", split_axis=0, concat_axis=0, tiled=True,
    )

    par_spec = pl.BlockSpec((per, 4 * MODES, LANES), lambda i: (i, 2, 0))
    quad = pl.BlockSpec((per, STEPS, SEGS, LANES), lambda i: (i, 0, 0, 0))
    segq = pl.BlockSpec((per, SEGS, MODES, LANES), lambda i: (i, 0, 0, 0))
    inner, seg_states = pl.pallas_call(
        inner_kernel,
        grid=(grid,),
        in_specs=[pl.BlockSpec((per, CHUNK, LANES), lambda i: (i, 0, 0)), par_spec, full],
        out_specs=[quad, segq],
        out_shape=[
            jax.ShapeDtypeStruct((groups, STEPS, SEGS, LANES), F32),
            jax.ShapeDtypeStruct((groups, SEGS, MODES, LANES), F32),
        ],
        scratch_shapes=[pltpu.VMEM((CHUNK, LANES), F32), pltpu.VMEM((MODES * SEGS, LANES), F32)],
        cost_estimate=cost(2_000_000_000, 6_000_000),
        interpret=interpret,
        name="inner",
    )(send, got, end_state)

    place = lax.axis_index("seq").astype(jnp.int32)[None]
    starts = pl.pallas_call(
        link_kernel,
        in_specs=[
            pl.BlockSpec(memory_space=pltpu.SMEM),
            pl.BlockSpec((groups, MODES, LANES), lambda: (0, 0, 0)),
            pl.BlockSpec((nseq, MODES, LANES), lambda: (0, 0, 0)),
            pl.BlockSpec((MODES, LANES), lambda: (0, 0)),
        ],
        out_specs=pl.BlockSpec((groups, MODES, LANES), lambda: (0, 0, 0)),
        out_shape=jax.ShapeDtypeStruct((groups, MODES, LANES), BF16),
        cost_estimate=cost(300_000, 500_000),
        interpret=interpret,
        name="link",
    )(place, before, blocks, decay_rate)

    mine = lax.all_to_all(starts, "ctx", split_axis=0, concat_axis=0, tiled=True)

    return pl.pallas_call(
        final_kernel,
        grid=(grid,),
        in_specs=[
            pl.BlockSpec((per, MODES, LANES), lambda i: (i, 0, 0)), par_spec, quad, segq, wide,
        ],
        out_specs=wide,
        out_shape=jax.ShapeDtypeStruct((tokens, channels), BF16),
        scratch_shapes=[pltpu.VMEM((MODES * SEGS, LANES), F32), pltpu.VMEM((CHUNK, LANES), F32)],
        cost_estimate=cost(20_000_000, 7_000_000),
        interpret=interpret,
        name="final",
    )(mine, got, inner, seg_states, queries)


def solution(mesh):
    rows = P(("seq", "ctx"), None)
    return jax.shard_map(
        local,
        mesh=mesh,
        in_specs=(rows, rows, rows, P(None, "ctx"), P(None, "ctx"), P("ctx")),
        out_specs=rows,
        check_vma=False,
    )
```

```python
import functools

import jax
import jax.numpy as jnp
from jax import lax
from jax.experimental import pallas as pl
from jax.experimental.pallas import tpu as pltpu
from jax.sharding import PartitionSpec as P

F32, BF16 = jnp.float32, jnp.bfloat16
LANES = 128
SUB = 8
CHUNK = 128
SEGS = 8
STEPS = CHUNK // SEGS
MODES = 16
TABLE = 3 * MODES + STEPS


def one_minus_exp(x):
    series = jnp.ones_like(x)
    for order in range(9, 1, -1):
        series = 1.0 - x * (1.0 / order) * series
    return jnp.where(x < 0.5, x * series, 1.0 - jnp.exp(-x))


def pack_kernel(k_ref, v_ref, rate_ref, resid_ref, gain_ref, out_ref, table_ref):
    @pl.when(pl.program_id(0) == 0)
    def _():
        rate = rate_ref[...]
        weight = resid_ref[...] * jnp.sqrt(one_minus_exp(2.0 * rate))
        power = jnp.exp(-rate)
        table_ref[0:16, :] = power
        table_ref[16:32, :] = weight * power
        table_ref[32:48, :] = jnp.exp(-float(STEPS) * rate)
        term = weight
        for lag in range(STEPS):
            tap = jnp.sum(term, axis=0, keepdims=True)
            table_ref[48 + lag : 49 + lag, :] = tap + gain_ref[...] if lag == 0 else tap
            term = term * power

    for g in range(out_ref.shape[0]):
        cols = slice(g * LANES, (g + 1) * LANES)
        out_ref[g] = (k_ref[:, cols].astype(F32) * v_ref[:, cols].astype(F32)).astype(BF16)


def states_kernel(in_ref, rate_ref, before_ref, end_ref, sig, ends):
    step = pl.program_id(0)
    nchunks = before_ref.shape[0]
    for i in range(SUB):
        sig[i * CHUNK : (i + 1) * CHUNK, :] = in_ref[i].astype(F32)
    power = jnp.exp(-rate_ref[...])
    powers = [jnp.broadcast_to(power[m : m + 1, :], (SUB, LANES)) for m in range(MODES)]

    def token(t, states):
        x = sig[pl.ds(t, SUB, stride=CHUNK), :]
        return tuple(powers[m] * states[m] + x for m in range(MODES))

    zero = jnp.zeros((SUB, LANES), F32)
    states = lax.fori_loop(0, CHUNK, token, (zero,) * MODES, unroll=8)
    for m in range(MODES):
        ends[pl.ds(pl.multiple_of(m * nchunks + step * SUB, SUB), SUB), :] = states[m]

    @pl.when(step == pl.num_programs(0) - 1)
    def _():
        decay = jnp.exp(-float(CHUNK) * rate_ref[...])
        state = jnp.zeros((MODES, LANES), F32)
        for d in range(nchunks):
            before_ref[d] = state
            state = decay * state + ends[pl.ds(d, MODES, stride=nchunks), :]
        for z in range(end_ref.shape[0]):
            end_ref[z] = state


def inner_kernel(send_ref, par_ref, y_ref, seg_ref, sig, ends):
    def group(g, carry):
        sig[...] = send_ref[g].astype(F32)
        power = par_ref[g, 0:16, :]
        taps = par_ref[g, 48:64, :]
        xs = [sig[pl.ds(t, SEGS, stride=STEPS), :] for t in range(STEPS)]
        tap = [jnp.broadcast_to(taps[j : j + 1, :], (SEGS, LANES)) for j in range(STEPS)]
        for t in range(STEPS):
            acc = tap[0] * xs[t]
            for j in range(1, t + 1):
                acc = acc + tap[j] * xs[t - j]
            y_ref[g, t] = acc
        for m in range(MODES):
            a = jnp.broadcast_to(power[m : m + 1, :], (SEGS, LANES))
            state = xs[0]
            for t in range(1, STEPS):
                state = a * state + xs[t]
            ends[m * SEGS : (m + 1) * SEGS, :] = state
        lift = par_ref[g, 16:32, :]
        decay = par_ref[g, 32:48, :]
        state = jnp.zeros((MODES, LANES), F32)
        for i in range(SEGS):
            seg_ref[g, i] = lift * state
            state = decay * state + ends[pl.ds(i, MODES, stride=SEGS), :]
        return carry

    lax.fori_loop(0, send_ref.shape[0], group, 0)


def link_kernel(place_ref, before_ref, blocks_ref, rate_ref, out_ref):
    nchunks = before_ref.shape[0]
    place = place_ref[0]
    span = jnp.exp(-float(CHUNK * nchunks) * rate_ref[...])
    start = jnp.zeros((MODES, LANES), F32)
    for z in range(blocks_ref.shape[0]):
        start = jnp.where(z < place, span * start + blocks_ref[z], start)
    decay = jnp.exp(-float(CHUNK) * rate_ref[...])
    for d in range(nchunks):
        out_ref[d] = (before_ref[d] + start).astype(BF16)
        start = decay * start


def final_kernel(start_ref, par_ref, y_ref, seg_ref, q_ref, out_ref, segs, pre):
    for g in range(y_ref.shape[0]):
        power = par_ref[g, 0:16, :]
        decay = par_ref[g, 32:48, :]
        lifted = par_ref[g, 16:32, :] * start_ref[g].astype(F32)
        for i in range(SEGS):
            segs[pl.ds(i, MODES, stride=SEGS), :] = seg_ref[g, i] + lifted
            lifted = lifted * decay
        terms = [segs[m * SEGS : (m + 1) * SEGS, :] for m in range(MODES)]
        powers = [jnp.broadcast_to(power[m : m + 1, :], (SEGS, LANES)) for m in range(MODES)]
        for t in range(STEPS):
            layer = list(terms)
            while len(layer) > 1:
                layer = [layer[i] + layer[i + 1] for i in range(0, len(layer), 2)]
            pre[pl.ds(t, SEGS, stride=STEPS), :] = y_ref[g, t] + layer[0]
            if t < STEPS - 1:
                terms = [terms[m] * powers[m] for m in range(MODES)]
        cols = slice(g * LANES, (g + 1) * LANES)
        gate = pre[...].astype(BF16).astype(F32)
        out_ref[:, cols] = (q_ref[:, cols].astype(F32) * gate).astype(BF16)


def cost(flops, nbytes):
    return pl.CostEstimate(flops=flops, bytes_accessed=nbytes, transcendentals=0)


def local(queries, key_proj, value_proj, decay_rate, residue, skip_gain, *, interpret=False):
    tokens, channels = queries.shape
    groups = channels // LANES
    per = 8
    params = pltpu.CompilerParams(vmem_limit_bytes=16 * 1024 * 1024)
    grid = groups // per
    full = pl.BlockSpec((MODES, LANES), lambda i: (0, 0))
    wide = pl.BlockSpec((CHUNK, per * LANES), lambda i: (0, i))
    state4 = jax.ShapeDtypeStruct((groups, MODES, LANES), F32)

    nseq = lax.axis_size("seq")
    tile = pl.BlockSpec((per, CHUNK, LANES), lambda i: (i, 0, 0))

    send, table = pl.pallas_call(
        pack_kernel,
        grid=(grid,),
        in_specs=[wide, wide, full, full, pl.BlockSpec((1, LANES), lambda i: (0, 0))],
        out_specs=[tile, pl.BlockSpec((TABLE, LANES), lambda i: (0, 0))],
        out_shape=[
            jax.ShapeDtypeStruct((groups, CHUNK, LANES), BF16),
            jax.ShapeDtypeStruct((TABLE, LANES), F32),
        ],
        cost_estimate=cost(1_000_000, 4_000_000),
        interpret=interpret,
        name="pack",
    )(key_proj, value_proj, decay_rate, residue, skip_gain[None, :])

    tables = lax.all_gather(table, "ctx", axis=0)
    got = lax.all_to_all(send, "ctx", split_axis=0, concat_axis=0, tiled=True)

    before, end_state = pl.pallas_call(
        states_kernel,
        grid=(groups // SUB,),
        in_specs=[pl.BlockSpec((SUB, CHUNK, LANES), lambda i: (i, 0, 0)), full],
        out_specs=[
            pl.BlockSpec((groups, MODES, LANES), lambda i: (0, 0, 0)),
            pl.BlockSpec((nseq, MODES, LANES), lambda i: (0, 0, 0)),
        ],
        out_shape=[state4, jax.ShapeDtypeStruct((nseq, MODES, LANES), F32)],
        scratch_shapes=[
            pltpu.VMEM((SUB * CHUNK, LANES), F32),
            pltpu.VMEM((MODES * groups, LANES), F32),
        ],
        cost_estimate=cost(20_000_000, 1_300_000),
        compiler_params=params,
        interpret=interpret,
        name="states",
    )(got, decay_rate)

    blocks = lax.all_to_all(end_state, "seq", split_axis=0, concat_axis=0, tiled=True)

    par_spec = pl.BlockSpec((per, TABLE, LANES), lambda i: (i, 0, 0))
    quad = pl.BlockSpec((per, STEPS, SEGS, LANES), lambda i: (i, 0, 0, 0))
    segq = pl.BlockSpec((per, SEGS, MODES, LANES), lambda i: (i, 0, 0, 0))
    inner, seg_states = pl.pallas_call(
        inner_kernel,
        grid=(grid,),
        in_specs=[tile, par_spec],
        out_specs=[quad, segq],
        out_shape=[
            jax.ShapeDtypeStruct((groups, STEPS, SEGS, LANES), F32),
            jax.ShapeDtypeStruct((groups, SEGS, MODES, LANES), F32),
        ],
        scratch_shapes=[pltpu.VMEM((CHUNK, LANES), F32), pltpu.VMEM((MODES * SEGS, LANES), F32)],
        cost_estimate=cost(2_000_000_000, 6_000_000),
        interpret=interpret,
        name="inner",
    )(send, tables)

    place = lax.axis_index("seq").astype(jnp.int32)[None]
    starts = pl.pallas_call(
        link_kernel,
        in_specs=[
            pl.BlockSpec(memory_space=pltpu.SMEM),
            pl.BlockSpec((groups, MODES, LANES), lambda: (0, 0, 0)),
            pl.BlockSpec((nseq, MODES, LANES), lambda: (0, 0, 0)),
            pl.BlockSpec((MODES, LANES), lambda: (0, 0)),
        ],
        out_specs=pl.BlockSpec((groups, MODES, LANES), lambda: (0, 0, 0)),
        out_shape=jax.ShapeDtypeStruct((groups, MODES, LANES), BF16),
        cost_estimate=cost(300_000, 500_000),
        compiler_params=params,
        interpret=interpret,
        name="link",
    )(place, before, blocks, decay_rate)

    mine = lax.all_to_all(starts, "ctx", split_axis=0, concat_axis=0, tiled=True)

    return pl.pallas_call(
        final_kernel,
        grid=(grid,),
        in_specs=[
            pl.BlockSpec((per, MODES, LANES), lambda i: (i, 0, 0)), par_spec, quad, segq, wide,
        ],
        out_specs=wide,
        out_shape=jax.ShapeDtypeStruct((tokens, channels), BF16),
        scratch_shapes=[pltpu.VMEM((MODES * SEGS, LANES), F32), pltpu.VMEM((CHUNK, LANES), F32)],
        cost_estimate=cost(20_000_000, 7_000_000),
        interpret=interpret,
        name="final",
    )(mine, tables, inner, seg_states, queries)


def solution(mesh):
    rows = P(("seq", "ctx"), None)
    return jax.shard_map(
        local,
        mesh=mesh,
        in_specs=(rows, rows, rows, P(None, "ctx"), P(None, "ctx"), P("ctx")),
        out_specs=rows,
        check_vma=False,
    )
```

```python
import jax
import jax.numpy as jnp
from jax import lax
from jax.experimental import pallas as pl
from jax.experimental.pallas import tpu as pltpu
from jax.sharding import PartitionSpec as P

F32, BF16 = jnp.float32, jnp.bfloat16
LANES = 128
SUB = 8
WIDE = SUB * LANES
CHUNK = 128
MODES = 16
ROWS = 2 * MODES + SUB
TABLE = 2 * MODES + 1


def one_minus_exp(x):
    series = jnp.ones_like(x)
    for order in range(9, 1, -1):
        series = 1.0 - x * (1.0 / order) * series
    return jnp.where(x < 0.5, x * series, 1.0 - jnp.exp(-x))


def table_kernel(rate_ref, resid_ref, gain_ref, out_ref):
    rate = rate_ref[...]
    weight = resid_ref[...] * jnp.sqrt(one_minus_exp(2.0 * rate))
    gain = jnp.broadcast_to(gain_ref[...], (SUB, LANES))
    rows = jnp.concatenate([rate, weight, gain], axis=0).astype(BF16)
    for d in range(out_ref.shape[0]):
        out_ref[d] = rows


def mix_kernel(k_ref, v_ref, out_ref):
    for g in range(SUB):
        cols = slice(g * LANES, (g + 1) * LANES)
        mixed = k_ref[:, cols].astype(F32) * v_ref[:, cols].astype(F32)
        out_ref[pl.ds(g, CHUNK, stride=SUB), :] = mixed.astype(BF16).astype(F32)


def chunk_kernel(x_ref, par_ref, end_ref, table_ref, rows, ends):
    for g in range(SUB):
        rows[g * ROWS : g * ROWS + ROWS, :] = par_ref[g].astype(F32)
    powers = []
    for m in range(MODES):
        power = jnp.exp(-rows[pl.ds(m, SUB, stride=ROWS), :])
        powers.append(power)
        table_ref[m * SUB : (m + 1) * SUB, :] = power
        table_ref[(MODES + m) * SUB : (MODES + m + 1) * SUB, :] = rows[
            pl.ds(MODES + m, SUB, stride=ROWS), :
        ]
    table_ref[2 * MODES * SUB :, :] = rows[pl.ds(2 * MODES, SUB, stride=ROWS), :]

    def token(t, states):
        x = x_ref[pl.ds(pl.multiple_of(t * SUB, SUB), SUB), :]
        return tuple(powers[m] * states[m] + x for m in range(MODES))

    zero = jnp.zeros((SUB, LANES), F32)
    states = lax.fori_loop(0, CHUNK, token, (zero,) * MODES, unroll=8)
    for m in range(MODES):
        ends[pl.ds(m, SUB, stride=MODES), :] = states[m]
    for g in range(SUB):
        end_ref[g] = ends[g * MODES : (g + 1) * MODES, :].astype(BF16)


def tree_sum(terms):
    while len(terms) > 1:
        terms = [terms[i] + terms[i + 1] for i in range(0, len(terms), 2)]
    return terms[0]


def inner_kernel(x_ref, table_ref, y_ref):
    powers = [table_ref[m * SUB : (m + 1) * SUB, :] for m in range(MODES)]
    weights = [table_ref[(MODES + m) * SUB : (MODES + m + 1) * SUB, :] for m in range(MODES)]
    gain = table_ref[2 * MODES * SUB :, :]

    def token(t, states):
        at = pl.ds(pl.multiple_of(t * SUB, SUB), SUB)
        x = x_ref[at, :]
        states = tuple(powers[m] * states[m] + x for m in range(MODES))
        y_ref[at, :] = gain * x + tree_sum([weights[m] * states[m] for m in range(MODES)])
        return states

    zero = jnp.zeros((SUB, LANES), F32)
    lax.fori_loop(0, CHUNK, token, (zero,) * MODES, unroll=4)


def block_kernel(ends_ref, rate_ref, before_ref, end_ref):
    decay = jnp.exp(-float(CHUNK) * rate_ref[...])
    state = jnp.zeros((MODES, LANES), F32)
    for d in range(before_ref.shape[0]):
        before_ref[d] = state
        state = decay * state + ends_ref[d].astype(F32)
    for z in range(end_ref.shape[0]):
        end_ref[z] = state


def link_kernel(place_ref, before_ref, blocks_ref, rate_ref, out_ref):
    nchunks = before_ref.shape[0]
    place = place_ref[0]
    span = jnp.exp(-float(CHUNK * nchunks) * rate_ref[...])
    start = jnp.zeros((MODES, LANES), F32)
    for z in range(blocks_ref.shape[0]):
        start = jnp.where(z < place, span * start + blocks_ref[z], start)
    decay = jnp.exp(-float(CHUNK) * rate_ref[...])
    for d in range(nchunks):
        out_ref[d] = (before_ref[d] + start).astype(BF16)
        start = decay * start


def final_kernel(start_ref, table_ref, y_ref, q_ref, out_ref, rows, pre):
    for g in range(SUB):
        rows[g * MODES : (g + 1) * MODES, :] = start_ref[g].astype(F32)
    powers = [table_ref[m * SUB : (m + 1) * SUB, :] for m in range(MODES)]
    terms = tuple(
        table_ref[(MODES + m) * SUB : (MODES + m + 1) * SUB, :]
        * powers[m]
        * rows[pl.ds(m, SUB, stride=MODES), :]
        for m in range(MODES)
    )

    def token(t, terms):
        at = pl.ds(pl.multiple_of(t * SUB, SUB), SUB)
        pre[at, :] = y_ref[at, :] + tree_sum(list(terms))
        return tuple(terms[m] * powers[m] for m in range(MODES))

    lax.fori_loop(0, CHUNK, token, terms, unroll=8)
    for g in range(SUB):
        cols = slice(g * LANES, (g + 1) * LANES)
        gate = pre[pl.ds(g, CHUNK, stride=SUB), :].astype(BF16).astype(F32)
        out_ref[:, cols] = (q_ref[:, cols].astype(F32) * gate).astype(BF16)


def local(queries, key_proj, value_proj, decay_rate, residue, skip_gain, *, interpret=False):
    tokens, channels = queries.shape
    groups = channels // LANES
    grid = channels // WIDE
    nseq = lax.axis_size("seq")

    def call(kernel, name, flops, nbytes, **kw):
        return pl.pallas_call(
            kernel,
            name=name,
            cost_estimate=pl.CostEstimate(flops=flops, bytes_accessed=nbytes, transcendentals=0),
            interpret=interpret,
            **kw,
        )

    def exchange(array, axis):
        return lax.all_to_all(array, axis, split_axis=0, concat_axis=0, tiled=True)

    struct = jax.ShapeDtypeStruct
    tight = pltpu.CompilerParams(vmem_limit_bytes=16 * 1024 * 1024)
    cols = pl.BlockSpec((CHUNK, WIDE), lambda i: (0, i))
    rows = pl.BlockSpec((CHUNK * SUB, LANES), lambda i: (i, 0))
    modes = pl.BlockSpec((SUB, MODES, LANES), lambda i: (i, 0, 0))
    tables = pl.BlockSpec((TABLE * SUB, LANES), lambda i: (i, 0))
    signal = struct((grid * CHUNK * SUB, LANES), F32)

    params = call(
        table_kernel, "table", 1_000_000, 400_000,
        out_shape=struct((groups, ROWS, LANES), BF16),
    )(decay_rate, residue, skip_gain[None, :])
    params = exchange(params, "ctx")

    mixed = call(
        mix_kernel, "mix", 2_000_000_000, 4_000_000,
        grid=(grid,), in_specs=[cols, cols], out_specs=rows, out_shape=signal,
    )(key_proj, value_proj)

    ends, table = call(
        chunk_kernel, "chunk", 20_000_000, 3_000_000,
        grid=(grid,),
        in_specs=[rows, pl.BlockSpec((SUB, ROWS, LANES), lambda i: (i, 0, 0))],
        out_specs=[modes, tables],
        out_shape=[struct((groups, MODES, LANES), BF16), struct((grid * TABLE * SUB, LANES), F32)],
        scratch_shapes=[
            pltpu.VMEM((SUB * ROWS, LANES), F32),
            pltpu.VMEM((SUB * MODES, LANES), F32),
        ],
    )(mixed, params)
    ends = exchange(ends, "ctx")

    before, end_state = call(
        block_kernel, "block", 300_000, 500_000,
        out_shape=[struct((groups, MODES, LANES), F32), struct((nseq, MODES, LANES), F32)],
        compiler_params=tight,
    )(ends, decay_rate)
    blocks = exchange(end_state, "seq")

    inner = call(
        inner_kernel, "inner", 2_000_000_000, 5_000_000,
        grid=(grid,), in_specs=[rows, tables], out_specs=rows, out_shape=signal,
    )(mixed, table)

    starts = call(
        link_kernel, "link", 300_000, 500_000,
        in_specs=[pl.BlockSpec(memory_space=pltpu.SMEM)] + [pl.BlockSpec(memory_space=pltpu.VMEM)] * 3,
        out_shape=struct((groups, MODES, LANES), BF16),
        compiler_params=tight,
    )(lax.axis_index("seq").astype(jnp.int32)[None], before, blocks, decay_rate)
    starts = exchange(starts, "ctx")

    return call(
        final_kernel, "final", 20_000_000, 5_000_000,
        grid=(grid,),
        in_specs=[modes, tables, rows, cols],
        out_specs=cols,
        out_shape=struct((tokens, channels), BF16),
        scratch_shapes=[
            pltpu.VMEM((SUB * MODES, LANES), F32),
            pltpu.VMEM((CHUNK * SUB, LANES), F32),
        ],
    )(starts, table, inner, queries)


def solution(mesh):
    rows = P(("seq", "ctx"), None)
    return jax.shard_map(
        local,
        mesh=mesh,
        in_specs=(rows, rows, rows, P(None, "ctx"), P(None, "ctx"), P("ctx")),
        out_specs=rows,
        check_vma=False,
    )
```

```python
import jax
import jax.numpy as jnp
from jax import lax
from jax.experimental import pallas as pl
from jax.experimental.pallas import tpu as pltpu
from jax.sharding import PartitionSpec as P

F32, BF16 = jnp.float32, jnp.bfloat16
LANES = 128
SUB = 8
WIDE = SUB * LANES
CHUNK = 128
MODES = 16
ROWS = 2 * MODES + SUB


def one_minus_exp(x):
    series = jnp.ones_like(x)
    for order in range(9, 1, -1):
        series = 1.0 - x * (1.0 / order) * series
    return jnp.where(x < 0.5, x * series, 1.0 - jnp.exp(-x))


def table_kernel(rate_ref, resid_ref, gain_ref, out_ref):
    rate = rate_ref[...]
    weight = resid_ref[...] * jnp.sqrt(one_minus_exp(2.0 * rate))
    gain = jnp.broadcast_to(gain_ref[...], (SUB, LANES))
    rows = jnp.concatenate([rate, weight, gain], axis=0).astype(BF16)
    for d in range(out_ref.shape[0]):
        out_ref[d] = rows


def mix_kernel(k_ref, v_ref, out_ref):
    for g in range(SUB):
        cols = slice(g * LANES, (g + 1) * LANES)
        mixed = k_ref[:, cols].astype(F32) * v_ref[:, cols].astype(F32)
        out_ref[pl.ds(g, CHUNK, stride=SUB), :] = mixed.astype(BF16).astype(F32)


def spread(par_ref, first, rows):
    for g in range(SUB):
        rows[g * ROWS : g * ROWS + ROWS, :] = par_ref[first + g].astype(F32)


def chunk_kernel(x_ref, par_ref, end_ref, rows, ends):
    for wide in range(x_ref.shape[0] // (CHUNK * SUB)):
        place = wide * CHUNK * SUB
        spread(par_ref, wide * SUB, rows)
        powers = [jnp.exp(-rows[pl.ds(m, SUB, stride=ROWS), :]) for m in range(MODES)]

        def token(t, states):
            x = x_ref[pl.ds(pl.multiple_of(place + t * SUB, SUB), SUB), :]
            return tuple(powers[m] * states[m] + x for m in range(MODES))

        zero = jnp.zeros((SUB, LANES), F32)
        states = lax.fori_loop(0, CHUNK, token, (zero,) * MODES, unroll=8)
        for m in range(MODES):
            ends[pl.ds(m, SUB, stride=MODES), :] = states[m]
        for g in range(SUB):
            end_ref[wide * SUB + g] = ends[g * MODES : (g + 1) * MODES, :].astype(BF16)


def tree_sum(terms):
    while len(terms) > 1:
        terms = [terms[i] + terms[i + 1] for i in range(0, len(terms), 2)]
    return terms[0]


def inner_kernel(x_ref, par_ref, y_ref, rows):
    spread(par_ref, 0, rows)
    powers = [jnp.exp(-rows[pl.ds(m, SUB, stride=ROWS), :]) for m in range(MODES)]
    weights = [rows[pl.ds(MODES + m, SUB, stride=ROWS), :] for m in range(MODES)]
    gain = rows[pl.ds(2 * MODES, SUB, stride=ROWS), :]

    def token(t, states):
        at = pl.ds(pl.multiple_of(t * SUB, SUB), SUB)
        x = x_ref[at, :]
        states = tuple(powers[m] * states[m] + x for m in range(MODES))
        y_ref[at, :] = gain * x + tree_sum([weights[m] * states[m] for m in range(MODES)])
        return states

    zero = jnp.zeros((SUB, LANES), F32)
    lax.fori_loop(0, CHUNK, token, (zero,) * MODES, unroll=4)


def block_kernel(ends_ref, rate_ref, before_ref, end_ref):
    decay = jnp.exp(-float(CHUNK) * rate_ref[...])
    state = jnp.zeros((MODES, LANES), F32)
    for d in range(before_ref.shape[0]):
        before_ref[d] = state
        state = decay * state + ends_ref[d].astype(F32)
    for z in range(end_ref.shape[0]):
        end_ref[z] = state


def link_kernel(place_ref, before_ref, blocks_ref, rate_ref, out_ref):
    nchunks = before_ref.shape[0]
    place = place_ref[0]
    span = jnp.exp(-float(CHUNK * nchunks) * rate_ref[...])
    start = jnp.zeros((MODES, LANES), F32)
    for z in range(blocks_ref.shape[0]):
        start = jnp.where(z < place, span * start + blocks_ref[z], start)
    decay = jnp.exp(-float(CHUNK) * rate_ref[...])
    for d in range(nchunks):
        out_ref[d] = (before_ref[d] + start).astype(BF16)
        start = decay * start


def final_kernel(start_ref, par_ref, y_ref, q_ref, out_ref, rows, starts, pre):
    spread(par_ref, 0, rows)
    for g in range(SUB):
        starts[g * MODES : (g + 1) * MODES, :] = start_ref[g].astype(F32)
    powers = [jnp.exp(-rows[pl.ds(m, SUB, stride=ROWS), :]) for m in range(MODES)]
    terms = tuple(
        rows[pl.ds(MODES + m, SUB, stride=ROWS), :]
        * powers[m]
        * starts[pl.ds(m, SUB, stride=MODES), :]
        for m in range(MODES)
    )

    def token(t, terms):
        at = pl.ds(pl.multiple_of(t * SUB, SUB), SUB)
        pre[at, :] = y_ref[at, :] + tree_sum(list(terms))
        return tuple(terms[m] * powers[m] for m in range(MODES))

    lax.fori_loop(0, CHUNK, token, terms, unroll=8)
    for g in range(SUB):
        cols = slice(g * LANES, (g + 1) * LANES)
        gate = pre[pl.ds(g, CHUNK, stride=SUB), :].astype(BF16).astype(F32)
        out_ref[:, cols] = (q_ref[:, cols].astype(F32) * gate).astype(BF16)


def local(queries, key_proj, value_proj, decay_rate, residue, skip_gain, *, interpret=False):
    tokens, channels = queries.shape
    groups = channels // LANES
    grid = channels // WIDE
    nseq = lax.axis_size("seq")

    def call(kernel, name, flops, nbytes, **kw):
        return pl.pallas_call(
            kernel,
            name=name,
            cost_estimate=pl.CostEstimate(flops=flops, bytes_accessed=nbytes, transcendentals=0),
            interpret=interpret,
            **kw,
        )

    def exchange(array, axis):
        return lax.all_to_all(array, axis, split_axis=0, concat_axis=0, tiled=True)

    struct = jax.ShapeDtypeStruct
    tight = pltpu.CompilerParams(vmem_limit_bytes=16 * 1024 * 1024)
    cols = pl.BlockSpec((CHUNK, WIDE), lambda i: (0, i))
    rows = pl.BlockSpec((CHUNK * SUB, LANES), lambda i: (i, 0))
    modes = pl.BlockSpec((SUB, MODES, LANES), lambda i: (i, 0, 0))
    tables = pl.BlockSpec((SUB, ROWS, LANES), lambda i: (i, 0, 0))
    signal = struct((grid * CHUNK * SUB, LANES), F32)

    params = call(
        table_kernel, "table", 1_000_000, 400_000,
        out_shape=struct((groups, ROWS, LANES), BF16),
    )(decay_rate, residue, skip_gain[None, :])
    params = exchange(params, "ctx")

    mixed = call(
        mix_kernel, "mix", 2_000_000_000, 4_000_000,
        grid=(grid,), in_specs=[cols, cols], out_specs=rows, out_shape=signal, compiler_params=tight,
    )(key_proj, value_proj)

    ends = call(
        chunk_kernel, "chunk", 20_000_000, 3_000_000,
        in_specs=[pl.BlockSpec(memory_space=pltpu.VMEM)] * 2,
        out_specs=pl.BlockSpec(memory_space=pltpu.VMEM),
        out_shape=struct((groups, MODES, LANES), BF16),
        scratch_shapes=[
            pltpu.VMEM((SUB * ROWS, LANES), F32),
            pltpu.VMEM((SUB * MODES, LANES), F32),
        ],
        compiler_params=tight,
    )(mixed, params)
    ends = exchange(ends, "ctx")

    before, end_state = call(
        block_kernel, "block", 300_000, 500_000,
        out_shape=[struct((groups, MODES, LANES), F32), struct((nseq, MODES, LANES), F32)],
        compiler_params=tight,
    )(ends, decay_rate)
    blocks = exchange(end_state, "seq")

    inner = call(
        inner_kernel, "inner", 2_000_000_000, 5_000_000,
        grid=(grid,),
        in_specs=[rows, tables],
        out_specs=rows,
        out_shape=pltpu.HBM(signal.shape, F32),
        scratch_shapes=[pltpu.VMEM((SUB * ROWS, LANES), F32)],
        compiler_params=tight,
    )(mixed, params)

    starts = call(
        link_kernel, "link", 300_000, 500_000,
        in_specs=[pl.BlockSpec(memory_space=pltpu.SMEM)] + [pl.BlockSpec(memory_space=pltpu.VMEM)] * 3,
        out_shape=struct((groups, MODES, LANES), BF16),
        compiler_params=tight,
    )(lax.axis_index("seq").astype(jnp.int32)[None], before, blocks, decay_rate)
    starts = exchange(starts, "ctx")

    return call(
        final_kernel, "final", 20_000_000, 5_000_000,
        grid=(grid,),
        in_specs=[modes, tables, rows, cols],
        out_specs=cols,
        out_shape=struct((tokens, channels), BF16),
        scratch_shapes=[
            pltpu.VMEM((SUB * ROWS, LANES), F32),
            pltpu.VMEM((SUB * MODES, LANES), F32),
            pltpu.VMEM((CHUNK * SUB, LANES), F32),
        ],
        compiler_params=tight,
    )(starts, params, pltpu.with_memory_space_constraint(inner, pltpu.HBM), queries)


def solution(mesh):
    rows = P(("seq", "ctx"), None)
    return jax.shard_map(
        local,
        mesh=mesh,
        in_specs=(rows, rows, rows, P(None, "ctx"), P(None, "ctx"), P("ctx")),
        out_specs=rows,
        check_vma=False,
    )
```

```python
import jax
import jax.numpy as jnp
import ml_dtypes
import numpy as np
from jax import lax
from jax.experimental import pallas as pl
from jax.experimental.pallas import tpu as pltpu
from jax.sharding import PartitionSpec as P

F32, BF16 = jnp.float32, jnp.bfloat16
LANES = 128
SUB = 8
WIDE = SUB * LANES
CHUNK = 128
MODES = 16
NODES = 23
SAMPLES = 24
ROWS = SAMPLES + 2 * MODES
GAIN = SAMPLES - 1


def node_tables():
    half = (CHUNK - 1) / 2.0
    nodes = half + half * np.cos((2.0 * np.arange(NODES) + 1.0) * np.pi / (2.0 * NODES))
    at = np.arange(CHUNK, dtype=np.float64)
    basis = np.zeros((SAMPLES, CHUNK))
    for k in range(NODES):
        others = np.delete(nodes, k)
        basis[k] = np.prod((at[:, None] - others) / (nodes[k] - others), axis=1)
    parts, left = [], basis
    for _ in range(3):
        part = left.astype(ml_dtypes.bfloat16)
        parts.append(part)
        left = left - part.astype(np.float64)
    column = np.concatenate([nodes, np.zeros(SAMPLES - NODES)]).astype(np.float32)
    return [float(n) for n in nodes], np.broadcast_to(column[:, None], (SAMPLES, LANES)), np.concatenate(parts)


def one_minus_exp(x):
    series = jnp.ones_like(x)
    for order in range(9, 1, -1):
        series = 1.0 - x * (1.0 / order) * series
    return jnp.where(x < 0.5, x * series, 1.0 - jnp.exp(-x))


def mode_weights(rate, resid):
    return resid * jnp.sqrt(one_minus_exp(2.0 * rate))


def product(k, v):
    return (k.astype(F32) * v.astype(F32)).astype(BF16)


def tree_sum(terms):
    while len(terms) > 1:
        pairs = [terms[i] + terms[i + 1] for i in range(0, len(terms) - 1, 2)]
        terms = pairs + terms[len(terms) - len(terms) % 2 :]
    return terms[0]


def moments_kernel(k_ref, v_ref, basis_ref, rate_ref, resid_ref, gain_ref, out_ref, par):
    @pl.when(pl.program_id(0) == 0)
    def _():
        rate = rate_ref[...]
        par[0:MODES, :] = rate
        par[MODES : 2 * MODES, :] = mode_weights(rate, resid_ref[...])

    sums = jnp.dot(basis_ref[...], product(k_ref[...], v_ref[...]), preferred_element_type=F32)
    sums = sums[0:SAMPLES] + sums[SAMPLES : 2 * SAMPLES] + sums[2 * SAMPLES :]
    spot = lax.broadcasted_iota(jnp.int32, (SAMPLES, LANES), 0) == GAIN
    gain = jnp.broadcast_to(gain_ref[...], (SAMPLES, LANES))
    for g in range(SUB):
        part = jnp.where(spot, gain, sums[:, g * LANES : (g + 1) * LANES])
        out_ref[g] = jnp.concatenate([part, par[...]], axis=0).astype(BF16)


def mix_kernel(k_ref, v_ref, out_ref):
    for g in range(SUB):
        cols = slice(g * LANES, (g + 1) * LANES)
        out_ref[pl.ds(g, CHUNK, stride=SUB), :] = product(k_ref[:, cols], v_ref[:, cols]).astype(F32)


def block_kernel(nodes, got_ref, rate_ref, before_ref, end_ref):
    rate = rate_ref[...]
    decay = jnp.exp(-float(CHUNK) * rate)
    reach = [jnp.exp(-(CHUNK - 1.0 - node) * rate) for node in nodes]
    state = jnp.zeros((MODES, LANES), F32)
    for d in range(before_ref.shape[0]):
        before_ref[d] = state
        sums = got_ref[d].astype(F32)
        end = tree_sum(
            [reach[k] * jnp.broadcast_to(sums[k : k + 1, :], (MODES, LANES)) for k in range(NODES)]
        )
        state = decay * state + end
    for z in range(end_ref.shape[0]):
        end_ref[z] = state


def link_kernel(place_ref, before_ref, blocks_ref, rate_ref, resid_ref, column_ref, out_ref):
    nchunks = before_ref.shape[0]
    place = place_ref[0]
    rate = rate_ref[...]
    span = jnp.exp(-float(CHUNK * nchunks) * rate)
    start = jnp.zeros((MODES, LANES), F32)
    for z in range(blocks_ref.shape[0]):
        start = jnp.where(z < place, span * start + blocks_ref[z], start)
    decay = jnp.exp(-float(CHUNK) * rate)
    lift = mode_weights(rate, resid_ref[...]) * jnp.exp(-rate)
    column = column_ref[...]
    reach = [
        jnp.exp(-column * jnp.broadcast_to(rate[m : m + 1, :], (SAMPLES, LANES))) for m in range(MODES)
    ]
    for d in range(nchunks):
        lifted = lift * (before_ref[d] + start)
        out_ref[d] = tree_sum(
            [reach[m] * jnp.broadcast_to(lifted[m : m + 1, :], (SAMPLES, LANES)) for m in range(MODES)]
        ).astype(BF16)
        start = decay * start


def inner_kernel(x_ref, got_ref, y_ref, rows, wide):
    for g in range(SUB):
        rows[g * ROWS : (g + 1) * ROWS, :] = got_ref[g].astype(F32)

    def row(place):
        return rows[pl.ds(place, SUB, stride=ROWS), :]

    powers = [jnp.exp(-row(SAMPLES + m)) for m in range(MODES)]
    weights = [row(SAMPLES + MODES + m) for m in range(MODES)]
    gain = row(GAIN)

    def token(t, states):
        at = pl.ds(pl.multiple_of(t * SUB, SUB), SUB)
        x = x_ref[at, :]
        states = tuple(powers[m] * states[m] + x for m in range(MODES))
        wide[at, :] = gain * x + tree_sum([weights[m] * states[m] for m in range(MODES)])
        return states

    zero = jnp.zeros((SUB, LANES), F32)
    lax.fori_loop(0, CHUNK, token, (zero,) * MODES, unroll=4)
    for g in range(SUB):
        y_ref[:, g * LANES : (g + 1) * LANES] = wide[pl.ds(g, CHUNK, stride=SUB), :]


def final_kernel(start_ref, basis_ref, y_ref, q_ref, out_ref):
    values = jnp.concatenate([start_ref[g].astype(F32) for g in range(SUB)], axis=1)
    values = jnp.concatenate([values] * 3, axis=0).astype(BF16)
    pre = y_ref[...] + jnp.dot(basis_ref[...], values, preferred_element_type=F32)
    out_ref[...] = (q_ref[...].astype(F32) * pre.astype(BF16).astype(F32)).astype(BF16)


def local(queries, key_proj, value_proj, decay_rate, residue, skip_gain, *, interpret=False):
    tokens, channels = queries.shape
    groups = channels // LANES
    grid = channels // WIDE
    nseq = lax.axis_size("seq")
    nodes, column, basis = node_tables()

    def call(kernel, name, flops, nbytes, **kw):
        return pl.pallas_call(
            kernel,
            name=name,
            cost_estimate=pl.CostEstimate(flops=flops, bytes_accessed=nbytes, transcendentals=0),
            interpret=interpret,
            **kw,
        )

    def exchange(array, axis):
        return lax.all_to_all(array, axis, split_axis=0, concat_axis=0, tiled=True)

    struct = jax.ShapeDtypeStruct
    tight = pltpu.CompilerParams(vmem_limit_bytes=16 * 1024 * 1024)
    cols = pl.BlockSpec((CHUNK, WIDE), lambda i: (0, i))
    rows = pl.BlockSpec((CHUNK * SUB, LANES), lambda i: (i, 0))

    def fixed(*shape):
        return pl.BlockSpec(shape, lambda i: (0,) * len(shape))

    def stack(depth):
        return pl.BlockSpec((SUB, depth, LANES), lambda i: (i, 0, 0))

    sums = call(
        moments_kernel, "moments", 100_000_000, 3_000_000,
        grid=(grid,),
        in_specs=[
            cols, cols, fixed(3 * SAMPLES, CHUNK),
            fixed(MODES, LANES), fixed(MODES, LANES), fixed(1, LANES),
        ],
        out_specs=stack(ROWS),
        out_shape=struct((groups, ROWS, LANES), BF16),
        scratch_shapes=[pltpu.VMEM((2 * MODES, LANES), F32)],
    )(key_proj, value_proj, jnp.asarray(basis), decay_rate, residue, skip_gain[None, :])
    got = exchange(sums, "ctx")

    mixed = call(
        mix_kernel, "mix", 2_000_000_000, 4_000_000,
        grid=(grid,), in_specs=[cols, cols], out_specs=rows,
        out_shape=struct((grid * CHUNK * SUB, LANES), F32),
        compiler_params=tight,
    )(key_proj, value_proj)

    before, end_state = call(
        lambda *refs: block_kernel(nodes, *refs), "block", 300_000, 500_000,
        grid=(1,),
        in_specs=[fixed(groups, SAMPLES, LANES), fixed(MODES, LANES)],
        out_specs=[fixed(groups, MODES, LANES), fixed(nseq, MODES, LANES)],
        out_shape=[struct((groups, MODES, LANES), F32), struct((nseq, MODES, LANES), F32)],
        compiler_params=tight,
    )(got, decay_rate)
    blocks = exchange(end_state, "seq")

    inner = call(
        inner_kernel, "inner", 2_000_000_000, 5_000_000,
        grid=(grid,), in_specs=[rows, stack(ROWS)], out_specs=cols,
        out_shape=struct((tokens, channels), F32),
        scratch_shapes=[pltpu.VMEM((SUB * ROWS, LANES), F32), pltpu.VMEM((CHUNK * SUB, LANES), F32)],
        compiler_params=tight,
    )(mixed, got)

    starts = call(
        link_kernel, "link", 300_000, 500_000,
        in_specs=[pl.BlockSpec(memory_space=pltpu.SMEM)] + [pl.BlockSpec(memory_space=pltpu.VMEM)] * 5,
        out_shape=struct((groups, SAMPLES, LANES), BF16),
        compiler_params=tight,
    )(
        lax.axis_index("seq").astype(jnp.int32)[None],
        before, blocks, decay_rate, residue, jnp.asarray(column),
    )
    starts = exchange(starts, "ctx")

    return call(
        final_kernel, "final", 100_000_000, 5_000_000,
        grid=(grid,),
        in_specs=[stack(SAMPLES), fixed(CHUNK, 3 * SAMPLES), cols, cols],
        out_specs=cols,
        out_shape=struct((tokens, channels), BF16),
        compiler_params=tight,
    )(starts, jnp.asarray(basis.T), inner, queries)


def solution(mesh):
    rows = P(("seq", "ctx"), None)
    return jax.shard_map(
        local,
        mesh=mesh,
        in_specs=(rows, rows, rows, P(None, "ctx"), P(None, "ctx"), P("ctx")),
        out_specs=rows,
        check_vma=False,
    )
```

```python
import jax
import jax.numpy as jnp
import ml_dtypes
import numpy as np
from jax import lax
from jax.experimental import pallas as pl
from jax.experimental.pallas import tpu as pltpu
from jax.sharding import PartitionSpec as P

F32, BF16 = jnp.float32, jnp.bfloat16
LANES = 128
SUB = 8
WIDE = SUB * LANES
MANY = 16
CHUNK = 128
MODES = 16
NODES = 23
SAMPLES = 24
ROWS = SAMPLES + 2 * MODES
GAIN = SAMPLES - 1
ROOT_CTX, ROOT_SEQ = 21, 4
BLOCK_FLIP, GROUP_FLIP, HALF_FLIP = ROOT_CTX // SUB, ROOT_CTX % SUB, ROOT_CTX % MANY


def node_tables():
    half = (CHUNK - 1) / 2.0
    nodes = half + half * np.cos((2.0 * np.arange(NODES) + 1.0) * np.pi / (2.0 * NODES))
    at = np.arange(CHUNK, dtype=np.float64)
    basis = np.zeros((SAMPLES, CHUNK))
    for k in range(NODES):
        others = np.delete(nodes, k)
        basis[k] = np.prod((at[:, None] - others) / (nodes[k] - others), axis=1)
    parts, left = [], basis
    for _ in range(3):
        part = left.astype(ml_dtypes.bfloat16)
        parts.append(part)
        left = left - part.astype(np.float64)
    column = np.concatenate([nodes, np.zeros(SAMPLES - NODES)]).astype(np.float32)
    return [float(n) for n in nodes], np.broadcast_to(column[:, None], (SAMPLES, LANES)), np.concatenate(parts)


def one_minus_exp(x):
    series = jnp.ones_like(x)
    for order in range(9, 1, -1):
        series = 1.0 - x * (1.0 / order) * series
    return jnp.where(x < 0.5, x * series, 1.0 - jnp.exp(-x))


def mode_weights(rate, resid):
    return resid * jnp.sqrt(one_minus_exp(2.0 * rate))


def product(k, v):
    return (k.astype(F32) * v.astype(F32)).astype(BF16)


def tree_sum(terms):
    while len(terms) > 1:
        pairs = [terms[i] + terms[i + 1] for i in range(0, len(terms) - 1, 2)]
        terms = pairs + terms[len(terms) - len(terms) % 2 :]
    return terms[0]


def moments_kernel(k_ref, v_ref, basis_ref, rate_ref, resid_ref, gain_ref, out_ref, par):
    @pl.when(pl.program_id(0) == 0)
    def _():
        rate = rate_ref[...]
        par[0:MODES, :] = rate
        par[MODES : 2 * MODES, :] = mode_weights(rate, resid_ref[...])

    sums = jnp.dot(basis_ref[...], product(k_ref[...], v_ref[...]), preferred_element_type=F32)
    sums = sums[0:SAMPLES] + sums[SAMPLES : 2 * SAMPLES] + sums[2 * SAMPLES :]
    spot = lax.broadcasted_iota(jnp.int32, (SAMPLES, LANES), 0) == GAIN
    gain = jnp.broadcast_to(gain_ref[...], (SAMPLES, LANES))
    for g in range(MANY):
        part = jnp.where(spot, gain, sums[:, g * LANES : (g + 1) * LANES])
        out_ref[g ^ HALF_FLIP] = jnp.concatenate([part, par[...]], axis=0).astype(BF16)


def mix_kernel(k_ref, v_ref, out_ref):
    for g in range(SUB):
        cols = slice(g * LANES, (g + 1) * LANES)
        out_ref[pl.ds(g, CHUNK, stride=SUB), :] = product(k_ref[:, cols], v_ref[:, cols]).astype(F32)


def block_kernel(nodes, got_ref, rate_ref, after_ref, before_ref, end_ref):
    rate = rate_ref[...]
    decay = jnp.exp(-float(CHUNK) * rate)
    reach = [jnp.exp(-(CHUNK - 1.0 - node) * rate) for node in nodes]
    state = jnp.zeros((MODES, LANES), F32)
    for d in range(before_ref.shape[0]):
        before_ref[d] = state
        sums = got_ref[d ^ ROOT_CTX].astype(F32)
        end = tree_sum(
            [reach[k] * jnp.broadcast_to(sums[k : k + 1, :], (MODES, LANES)) for k in range(NODES)]
        )
        state = decay * state + end
    for z in range(end_ref.shape[0]):
        end_ref[z] = state


def link_kernel(place_ref, before_ref, blocks_ref, rate_ref, resid_ref, column_ref, after_ref, out_ref):
    nchunks = before_ref.shape[0]
    place = place_ref[0]
    rate = rate_ref[...]
    span = jnp.exp(-float(CHUNK * nchunks) * rate)
    start = jnp.zeros((MODES, LANES), F32)
    for z in range(blocks_ref.shape[0]):
        start = jnp.where(z < place, span * start + blocks_ref[z ^ ROOT_SEQ], start)
    decay = jnp.exp(-float(CHUNK) * rate)
    lift = mode_weights(rate, resid_ref[...]) * jnp.exp(-rate)
    column = column_ref[...]
    reach = [
        jnp.exp(-column * jnp.broadcast_to(rate[m : m + 1, :], (SAMPLES, LANES))) for m in range(MODES)
    ]
    for d in range(nchunks):
        lifted = lift * (before_ref[d] + start)
        out_ref[d ^ ROOT_CTX] = tree_sum(
            [reach[m] * jnp.broadcast_to(lifted[m : m + 1, :], (SAMPLES, LANES)) for m in range(MODES)]
        ).astype(BF16)
        start = decay * start


def inner_kernel(x_ref, got_ref, after_ref, held_ref, y_ref, rows, wide):
    for g in range(SUB):
        rows[g * ROWS : (g + 1) * ROWS, :] = got_ref[g ^ GROUP_FLIP].astype(F32)

    def row(place):
        return rows[pl.ds(place, SUB, stride=ROWS), :]

    powers = [jnp.exp(-row(SAMPLES + m)) for m in range(MODES)]
    weights = [row(SAMPLES + MODES + m) for m in range(MODES)]
    gain = row(GAIN)

    def token(t, states):
        at = pl.ds(pl.multiple_of(t * SUB, SUB), SUB)
        x = x_ref[at, :]
        states = tuple(powers[m] * states[m] + x for m in range(MODES))
        wide[at, :] = gain * x + tree_sum([weights[m] * states[m] for m in range(MODES)])
        return states

    zero = jnp.zeros((SUB, LANES), F32)
    lax.fori_loop(0, CHUNK, token, (zero,) * MODES, unroll=4)
    for g in range(SUB):
        y_ref[:, g * LANES : (g + 1) * LANES] = wide[pl.ds(g, CHUNK, stride=SUB), :]


def final_kernel(start_ref, basis_ref, y_ref, q_ref, out_ref):
    values = jnp.concatenate([start_ref[g ^ HALF_FLIP].astype(F32) for g in range(MANY)], axis=1)
    values = jnp.concatenate([values] * 3, axis=0).astype(BF16)
    pre = y_ref[...] + jnp.dot(basis_ref[...], values, preferred_element_type=F32)
    out_ref[...] = (q_ref[...].astype(F32) * pre.astype(BF16).astype(F32)).astype(BF16)


def local(queries, key_proj, value_proj, decay_rate, residue, skip_gain, *, interpret=False):
    tokens, channels = queries.shape
    groups = channels // LANES
    grid = channels // WIDE
    nseq = lax.axis_size("seq")
    nodes, column, basis = node_tables()

    def call(kernel, name, flops, nbytes, **kw):
        return pl.pallas_call(
            kernel,
            name=name,
            cost_estimate=pl.CostEstimate(flops=flops, bytes_accessed=nbytes, transcendentals=0),
            interpret=interpret,
            **kw,
        )

    def exchange(array, axis, root):
        order = [i ^ root for i in range(array.shape[0])]
        return lax.all_to_all(
            array, axis, split_axis=0, concat_axis=0, tiled=True, axis_index_groups=[order]
        )

    def in_hbm(array):
        return pltpu.with_memory_space_constraint(array, pltpu.HBM)

    struct = jax.ShapeDtypeStruct
    tight = pltpu.CompilerParams(vmem_limit_bytes=16 * 1024 * 1024)
    halves = pl.BlockSpec((CHUNK, MANY * LANES), lambda i: (0, i))
    anywhere = pl.BlockSpec(memory_space=pl.ANY)

    def fixed(*shape):
        return pl.BlockSpec(shape, lambda i: (0,) * len(shape))

    def stack(depth):
        return pl.BlockSpec((MANY, depth, LANES), lambda i: (i ^ (ROOT_CTX // MANY), 0, 0))

    sums = call(
        moments_kernel, "moments", 100_000_000, 3_000_000,
        grid=(2,),
        in_specs=[
            halves, halves, fixed(3 * SAMPLES, CHUNK),
            fixed(MODES, LANES), fixed(MODES, LANES), fixed(1, LANES),
        ],
        out_specs=stack(ROWS),
        out_shape=struct((groups, ROWS, LANES), BF16),
        scratch_shapes=[pltpu.VMEM((2 * MODES, LANES), F32)],
    )(key_proj, value_proj, jnp.asarray(basis), decay_rate, residue, skip_gain[None, :])
    got = exchange(sums, "ctx", ROOT_CTX)

    mixed = call(
        mix_kernel, "mix", 2_000_000_000, 4_000_000,
        grid=(grid,),
        in_specs=[pl.BlockSpec((CHUNK, WIDE), lambda i: (0, i))] * 2,
        out_specs=pl.BlockSpec((CHUNK * SUB, LANES), lambda i: (i, 0)),
        out_shape=struct((grid * CHUNK * SUB, LANES), F32),
        compiler_params=tight,
    )(in_hbm(key_proj), in_hbm(value_proj))

    before, end_state = call(
        lambda *refs: block_kernel(nodes, *refs), "block", 300_000, 500_000,
        grid=(1,),
        in_specs=[fixed(groups, SAMPLES, LANES), fixed(MODES, LANES), anywhere],
        out_specs=[fixed(groups, MODES, LANES), fixed(nseq, MODES, LANES)],
        out_shape=[struct((groups, MODES, LANES), F32), struct((nseq, MODES, LANES), F32)],
        compiler_params=tight,
    )(got, decay_rate, mixed)
    blocks = exchange(end_state, "seq", ROOT_SEQ)

    def respond(half, after, held):
        steps = grid // 2

        def at(i):
            return i + half * steps

        specs = [
            pl.BlockSpec((CHUNK * SUB, LANES), lambda i: (at(i), 0)),
            pl.BlockSpec((SUB, ROWS, LANES), lambda i: (at(i) ^ BLOCK_FLIP, 0, 0)),
            anywhere,
            anywhere,
        ]
        return call(
            inner_kernel, "inner", 1_000_000_000, 2_500_000,
            grid=(steps,), in_specs=specs,
            out_specs=pl.BlockSpec((CHUNK, WIDE), lambda i: (0, at(i))),
            out_shape=struct((tokens, channels), F32),
            scratch_shapes=[pltpu.VMEM((SUB * ROWS, LANES), F32), pltpu.VMEM((CHUNK * SUB, LANES), F32)],
            input_output_aliases={3: 0} if half else {},
            compiler_params=tight,
        )(mixed, got, after, held)

    inner = respond(0, end_state, end_state)

    starts = call(
        link_kernel, "link", 300_000, 500_000,
        in_specs=[pl.BlockSpec(memory_space=pltpu.SMEM)] + [pl.BlockSpec(memory_space=pltpu.VMEM)] * 5 + [anywhere],
        out_shape=struct((groups, SAMPLES, LANES), BF16),
        compiler_params=tight,
    )(
        lax.axis_index("seq").astype(jnp.int32)[None],
        before, blocks, decay_rate, residue, jnp.asarray(column), inner,
    )
    inner = respond(1, starts, inner)
    starts = exchange(starts, "ctx", ROOT_CTX)

    return call(
        final_kernel, "final", 100_000_000, 5_000_000,
        grid=(2,),
        in_specs=[stack(SAMPLES), fixed(CHUNK, 3 * SAMPLES), halves, halves],
        out_specs=halves,
        out_shape=struct((tokens, channels), BF16),
        compiler_params=tight,
    )(starts, jnp.asarray(basis.T), inner, in_hbm(queries))


def solution(mesh):
    rows = P(("seq", "ctx"), None)
    return jax.shard_map(
        local,
        mesh=mesh,
        in_specs=(rows, rows, rows, P(None, "ctx"), P(None, "ctx"), P("ctx")),
        out_specs=rows,
        check_vma=False,
    )
```

```python
import jax
import jax.numpy as jnp
import ml_dtypes
import numpy as np
from jax import lax
from jax.experimental import pallas as pl
from jax.experimental.pallas import tpu as pltpu
from jax.sharding import PartitionSpec as P

F32, BF16 = jnp.float32, jnp.bfloat16
LANES = 128
SUB = 8
WIDE = SUB * LANES
MANY = 16
CHUNK = 128
MODES = 16
NODES = 23
SAMPLES = 24
ROWS = SAMPLES + 2 * MODES
GAIN = SAMPLES - 1
ROOT_CTX, ROOT_SEQ = 21, 4
BLOCK_FLIP, GROUP_FLIP, HALF_FLIP = ROOT_CTX // SUB, ROOT_CTX % SUB, ROOT_CTX % MANY


def node_tables():
    half = (CHUNK - 1) / 2.0
    nodes = half + half * np.cos((2.0 * np.arange(NODES) + 1.0) * np.pi / (2.0 * NODES))
    at = np.arange(CHUNK, dtype=np.float64)
    basis = np.zeros((SAMPLES, CHUNK))
    for k in range(NODES):
        others = np.delete(nodes, k)
        basis[k] = np.prod((at[:, None] - others) / (nodes[k] - others), axis=1)
    parts, left = [], basis
    for _ in range(3):
        part = left.astype(ml_dtypes.bfloat16)
        parts.append(part)
        left = left - part.astype(np.float64)
    return [float(n) for n in nodes], np.concatenate(parts)


def one_minus_exp(x):
    series = jnp.ones_like(x)
    for order in range(9, 1, -1):
        series = 1.0 - x * (1.0 / order) * series
    return jnp.where(x < 0.5, x * series, 1.0 - jnp.exp(-x))


def mode_weights(rate, resid):
    return resid * jnp.sqrt(one_minus_exp(2.0 * rate))


def product(k, v):
    return (k.astype(F32) * v.astype(F32)).astype(BF16)


def tree_sum(terms):
    while len(terms) > 1:
        pairs = [terms[i] + terms[i + 1] for i in range(0, len(terms) - 1, 2)]
        terms = pairs + terms[len(terms) - len(terms) % 2 :]
    return terms[0]


def moments_kernel(k_ref, v_ref, basis_ref, rate_ref, resid_ref, gain_ref, out_ref, par):
    @pl.when(pl.program_id(0) == 0)
    def _():
        rate = rate_ref[...]
        par[0:MODES, :] = rate
        par[MODES : 2 * MODES, :] = mode_weights(rate, resid_ref[...])

    sums = jnp.dot(basis_ref[...], product(k_ref[...], v_ref[...]), preferred_element_type=F32)
    sums = sums[0:SAMPLES] + sums[SAMPLES : 2 * SAMPLES] + sums[2 * SAMPLES :]
    spot = lax.broadcasted_iota(jnp.int32, (SAMPLES, LANES), 0) == GAIN
    gain = jnp.broadcast_to(gain_ref[...], (SAMPLES, LANES))
    for g in range(MANY):
        part = jnp.where(spot, gain, sums[:, g * LANES : (g + 1) * LANES])
        out_ref[g ^ HALF_FLIP] = jnp.concatenate([part, par[...]], axis=0).astype(BF16)


def mix_kernel(k_ref, v_ref, out_ref):
    for g in range(SUB):
        cols = slice(g * LANES, (g + 1) * LANES)
        out_ref[pl.ds(g, CHUNK, stride=SUB), :] = product(k_ref[:, cols], v_ref[:, cols]).astype(F32)


def block_kernel(nodes, got_ref, rate_ref, after_ref, before_ref, end_ref):
    rate = rate_ref[...]
    decay = jnp.exp(-float(CHUNK) * rate)
    reach = [jnp.exp(-(CHUNK - 1.0 - node) * rate) for node in nodes]
    state = jnp.zeros((MODES, LANES), F32)
    for d in range(before_ref.shape[0]):
        before_ref[d] = state
        sums = got_ref[d ^ ROOT_CTX].astype(F32)
        end = tree_sum(
            [reach[k] * jnp.broadcast_to(sums[k : k + 1, :], (MODES, LANES)) for k in range(NODES)]
        )
        state = decay * state + end
    for z in range(end_ref.shape[0]):
        end_ref[z] = state


def link_kernel(nodes, place_ref, before_ref, blocks_ref, rate_ref, resid_ref, after_ref, out_ref):
    nchunks = before_ref.shape[0]
    place = place_ref[0]
    rate = rate_ref[...]
    span = jnp.exp(-float(CHUNK * nchunks) * rate)
    start = jnp.zeros((MODES, LANES), F32)
    for z in range(blocks_ref.shape[0]):
        start = jnp.where(z < place, span * start + blocks_ref[z ^ ROOT_SEQ], start)
    decay = jnp.exp(-float(CHUNK) * rate)
    lift = mode_weights(rate, resid_ref[...]) * jnp.exp(-rate)
    spot = lax.broadcasted_iota(jnp.int32, (SAMPLES, LANES), 0)
    column = jnp.zeros((SAMPLES, LANES), F32)
    for k, node in enumerate(nodes):
        column = jnp.where(spot == k, node, column)
    reach = [
        jnp.exp(-column * jnp.broadcast_to(rate[m : m + 1, :], (SAMPLES, LANES))) for m in range(MODES)
    ]
    for d in range(nchunks):
        lifted = lift * (before_ref[d] + start)
        out_ref[d ^ ROOT_CTX] = tree_sum(
            [reach[m] * jnp.broadcast_to(lifted[m : m + 1, :], (SAMPLES, LANES)) for m in range(MODES)]
        ).astype(BF16)
        start = decay * start


def inner_kernel(x_ref, got_ref, after_ref, held_ref, y_ref, rows, wide):
    for g in range(SUB):
        rows[g * ROWS : (g + 1) * ROWS, :] = got_ref[g ^ GROUP_FLIP].astype(F32)

    def row(place):
        return rows[pl.ds(place, SUB, stride=ROWS), :]

    powers = [jnp.exp(-row(SAMPLES + m)) for m in range(MODES)]
    weights = [row(SAMPLES + MODES + m) for m in range(MODES)]
    gain = row(GAIN)

    def token(t, states):
        at = pl.ds(pl.multiple_of(t * SUB, SUB), SUB)
        x = x_ref[at, :]
        states = tuple(powers[m] * states[m] + x for m in range(MODES))
        wide[at, :] = gain * x + tree_sum([weights[m] * states[m] for m in range(MODES)])
        return states

    zero = jnp.zeros((SUB, LANES), F32)
    lax.fori_loop(0, CHUNK, token, (zero,) * MODES, unroll=4)
    for g in range(SUB):
        y_ref[:, g * LANES : (g + 1) * LANES] = wide[pl.ds(g, CHUNK, stride=SUB), :]


def final_kernel(start_ref, basis_ref, y_ref, q_ref, out_ref):
    values = jnp.concatenate([start_ref[g ^ HALF_FLIP].astype(F32) for g in range(MANY)], axis=1)
    values = jnp.concatenate([values] * 3, axis=0).astype(BF16)
    pre = y_ref[...] + jnp.dot(basis_ref[...], values, preferred_element_type=F32)
    out_ref[...] = (q_ref[...].astype(F32) * pre.astype(BF16).astype(F32)).astype(BF16)


def local(queries, key_proj, value_proj, decay_rate, residue, skip_gain, *, interpret=False):
    tokens, channels = queries.shape
    groups = channels // LANES
    grid = channels // WIDE
    nseq = lax.axis_size("seq")
    nodes, basis = node_tables()

    def call(kernel, name, flops, nbytes, **kw):
        return pl.pallas_call(
            kernel,
            name=name,
            cost_estimate=pl.CostEstimate(flops=flops, bytes_accessed=nbytes, transcendentals=0),
            interpret=interpret,
            **kw,
        )

    def exchange(array, axis, root):
        order = [i ^ root for i in range(array.shape[0])]
        return lax.all_to_all(
            array, axis, split_axis=0, concat_axis=0, tiled=True, axis_index_groups=[order]
        )

    def in_hbm(array):
        return pltpu.with_memory_space_constraint(array, pltpu.HBM)

    struct = jax.ShapeDtypeStruct
    tight = pltpu.CompilerParams(vmem_limit_bytes=16 * 1024 * 1024)
    halves = pl.BlockSpec((CHUNK, MANY * LANES), lambda i: (0, i))
    anywhere = pl.BlockSpec(memory_space=pl.ANY)

    def fixed(*shape):
        return pl.BlockSpec(shape, lambda i: (0,) * len(shape))

    def stack(depth):
        return pl.BlockSpec((MANY, depth, LANES), lambda i: (i ^ (ROOT_CTX // MANY), 0, 0))

    sums = call(
        moments_kernel, "moments", 100_000_000, 3_000_000,
        grid=(2,),
        in_specs=[
            halves, halves, fixed(3 * SAMPLES, CHUNK),
            fixed(MODES, LANES), fixed(MODES, LANES), fixed(1, LANES),
        ],
        out_specs=stack(ROWS),
        out_shape=struct((groups, ROWS, LANES), BF16),
        scratch_shapes=[pltpu.VMEM((2 * MODES, LANES), F32)],
    )(key_proj, value_proj, jnp.asarray(basis), decay_rate, residue, skip_gain[None, :])
    got = exchange(sums, "ctx", ROOT_CTX)

    mixed = call(
        mix_kernel, "mix", 2_000_000_000, 4_000_000,
        grid=(grid,),
        in_specs=[pl.BlockSpec((CHUNK, WIDE), lambda i: (0, i))] * 2,
        out_specs=pl.BlockSpec((CHUNK * SUB, LANES), lambda i: (i, 0)),
        out_shape=pltpu.HBM((grid * CHUNK * SUB, LANES), F32),
    )(in_hbm(key_proj), in_hbm(value_proj))

    before, end_state = call(
        lambda *refs: block_kernel(nodes, *refs), "block", 300_000, 500_000,
        grid=(1,),
        in_specs=[fixed(groups, SAMPLES, LANES), fixed(MODES, LANES), anywhere],
        out_specs=[fixed(groups, MODES, LANES), fixed(nseq, MODES, LANES)],
        out_shape=[struct((groups, MODES, LANES), F32), struct((nseq, MODES, LANES), F32)],
        compiler_params=tight,
    )(got, decay_rate, in_hbm(mixed))
    blocks = exchange(end_state, "seq", ROOT_SEQ)

    def respond(half, after, held):
        steps = grid // 2

        def at(i):
            return i + half * steps

        specs = [
            pl.BlockSpec((CHUNK * SUB, LANES), lambda i: (at(i), 0)),
            pl.BlockSpec((SUB, ROWS, LANES), lambda i: (at(i) ^ BLOCK_FLIP, 0, 0)),
            anywhere,
            anywhere,
        ]
        return call(
            inner_kernel, "inner", 1_000_000_000, 2_500_000,
            grid=(steps,), in_specs=specs,
            out_specs=pl.BlockSpec((CHUNK, WIDE), lambda i: (0, at(i))),
            out_shape=struct((tokens, channels), F32),
            scratch_shapes=[pltpu.VMEM((SUB * ROWS, LANES), F32), pltpu.VMEM((CHUNK * SUB, LANES), F32)],
            input_output_aliases={3: 0} if half else {},
            compiler_params=tight,
        )(in_hbm(mixed), got, after, held)

    inner = respond(0, end_state, end_state)

    starts = call(
        lambda *refs: link_kernel(nodes, *refs), "link", 300_000, 500_000,
        in_specs=[pl.BlockSpec(memory_space=pltpu.SMEM)] + [pl.BlockSpec(memory_space=pltpu.VMEM)] * 4 + [anywhere],
        out_shape=struct((groups, SAMPLES, LANES), BF16),
        compiler_params=tight,
    )(
        lax.axis_index("seq").astype(jnp.int32)[None],
        before, blocks, decay_rate, residue, inner,
    )
    inner = respond(1, starts, inner)
    starts = exchange(starts, "ctx", ROOT_CTX)

    return call(
        final_kernel, "final", 100_000_000, 5_000_000,
        grid=(2,),
        in_specs=[stack(SAMPLES), fixed(CHUNK, 3 * SAMPLES), halves, halves],
        out_specs=halves,
        out_shape=struct((tokens, channels), BF16),
        compiler_params=tight,
    )(starts, jnp.asarray(basis.T), inner, in_hbm(queries))


def solution(mesh):
    rows = P(("seq", "ctx"), None)
    return jax.shard_map(
        local,
        mesh=mesh,
        in_specs=(rows, rows, rows, P(None, "ctx"), P(None, "ctx"), P("ctx")),
        out_specs=rows,
        check_vma=False,
    )
```

```python
import jax
import jax.numpy as jnp
import ml_dtypes
import numpy as np
from jax import lax
from jax.experimental import pallas as pl
from jax.experimental.pallas import tpu as pltpu
from jax.sharding import PartitionSpec as P

F32, BF16 = jnp.float32, jnp.bfloat16
LANES = 128
SUB = 8
WIDE = SUB * LANES
MANY = 16
CHUNK = 128
MODES = 16
NODES = 23
SAMPLES = 24
ROWS = SAMPLES + 2 * MODES
GAIN = SAMPLES - 1
ROOT_CTX, ROOT_SEQ = 21, 4
BLOCK_FLIP, GROUP_FLIP, HALF_FLIP = ROOT_CTX // SUB, ROOT_CTX % SUB, ROOT_CTX % MANY


def node_tables():
    half = (CHUNK - 1) / 2.0
    nodes = half + half * np.cos((2.0 * np.arange(NODES) + 1.0) * np.pi / (2.0 * NODES))
    at = np.arange(CHUNK, dtype=np.float64)
    basis = np.zeros((SAMPLES, CHUNK))
    for k in range(NODES):
        others = np.delete(nodes, k)
        basis[k] = np.prod((at[:, None] - others) / (nodes[k] - others), axis=1)
    parts, left = [], basis
    for _ in range(3):
        part = left.astype(ml_dtypes.bfloat16)
        parts.append(part)
        left = left - part.astype(np.float64)
    return [float(n) for n in nodes], np.concatenate(parts)


def one_minus_exp(x):
    series = jnp.ones_like(x)
    for order in range(9, 1, -1):
        series = 1.0 - x * (1.0 / order) * series
    return jnp.where(x < 0.5, x * series, 1.0 - jnp.exp(-x))


def mode_weights(rate, resid):
    return resid * jnp.sqrt(one_minus_exp(2.0 * rate))


def product(k, v):
    return (k.astype(F32) * v.astype(F32)).astype(BF16)


def tree_sum(terms):
    while len(terms) > 1:
        pairs = [terms[i] + terms[i + 1] for i in range(0, len(terms) - 1, 2)]
        terms = pairs + terms[len(terms) - len(terms) % 2 :]
    return terms[0]


def moments_kernel(k_ref, v_ref, basis_ref, rate_ref, resid_ref, gain_ref, out_ref, par):
    @pl.when(pl.program_id(0) == 0)
    def _():
        rate = rate_ref[...]
        par[0:MODES, :] = rate
        par[MODES : 2 * MODES, :] = mode_weights(rate, resid_ref[...])

    sums = jnp.dot(basis_ref[...], product(k_ref[...], v_ref[...]), preferred_element_type=F32)
    sums = sums[0:SAMPLES] + sums[SAMPLES : 2 * SAMPLES] + sums[2 * SAMPLES :]
    spot = lax.broadcasted_iota(jnp.int32, (SAMPLES, LANES), 0) == GAIN
    gain = jnp.broadcast_to(gain_ref[...], (SAMPLES, LANES))
    for g in range(MANY):
        part = jnp.where(spot, gain, sums[:, g * LANES : (g + 1) * LANES])
        out_ref[g ^ HALF_FLIP] = jnp.concatenate([part, par[...]], axis=0).astype(BF16)


def mix_kernel(k_ref, v_ref, out_ref, wide):
    for g in range(SUB):
        cols = slice(g * LANES, (g + 1) * LANES)
        wide[pl.ds(g, CHUNK, stride=SUB), :] = product(k_ref[:, cols], v_ref[:, cols]).astype(F32)
    out_ref[...] = wide[...].astype(BF16)


def block_kernel(nodes, got_ref, rate_ref, after_ref, also_ref, before_ref, end_ref):
    rate = rate_ref[...]
    decay = jnp.exp(-float(CHUNK) * rate)
    reach = [jnp.exp(-(CHUNK - 1.0 - node) * rate) for node in nodes]
    state = jnp.zeros((MODES, LANES), F32)
    for d in range(before_ref.shape[0]):
        before_ref[d] = state
        sums = got_ref[d ^ ROOT_CTX].astype(F32)
        end = tree_sum(
            [reach[k] * jnp.broadcast_to(sums[k : k + 1, :], (MODES, LANES)) for k in range(NODES)]
        )
        state = decay * state + end
    for z in range(end_ref.shape[0]):
        end_ref[z] = state


def link_kernel(nodes, place_ref, before_ref, blocks_ref, rate_ref, resid_ref, after_ref, out_ref):
    nchunks = before_ref.shape[0]
    place = place_ref[0]
    rate = rate_ref[...]
    span = jnp.exp(-float(CHUNK * nchunks) * rate)
    start = jnp.zeros((MODES, LANES), F32)
    for z in range(blocks_ref.shape[0]):
        start = jnp.where(z < place, span * start + blocks_ref[z ^ ROOT_SEQ], start)
    decay = jnp.exp(-float(CHUNK) * rate)
    lift = mode_weights(rate, resid_ref[...]) * jnp.exp(-rate)
    spot = lax.broadcasted_iota(jnp.int32, (SAMPLES, LANES), 0)
    column = jnp.zeros((SAMPLES, LANES), F32)
    for k, node in enumerate(nodes):
        column = jnp.where(spot == k, node, column)
    reach = [
        jnp.exp(-column * jnp.broadcast_to(rate[m : m + 1, :], (SAMPLES, LANES))) for m in range(MODES)
    ]
    for d in range(nchunks):
        lifted = lift * (before_ref[d] + start)
        out_ref[d ^ ROOT_CTX] = tree_sum(
            [reach[m] * jnp.broadcast_to(lifted[m : m + 1, :], (SAMPLES, LANES)) for m in range(MODES)]
        ).astype(BF16)
        start = decay * start


def inner_kernel(x_ref, got_ref, after_ref, y_ref, rows, wide):
    for g in range(SUB):
        rows[g * ROWS : (g + 1) * ROWS, :] = got_ref[g ^ GROUP_FLIP].astype(F32)

    def row(place):
        return rows[pl.ds(place, SUB, stride=ROWS), :]

    powers = [jnp.exp(-row(SAMPLES + m)) for m in range(MODES)]
    weights = [row(SAMPLES + MODES + m) for m in range(MODES)]
    gain = row(GAIN)

    def tokens(t, states):
        at = pl.multiple_of(t * 2 * SUB, 2 * SUB)
        pair = x_ref[pl.ds(at, 2 * SUB), :].astype(F32)
        outs = []
        for x in (pair[:SUB], pair[SUB:]):
            states = tuple(powers[m] * states[m] + x for m in range(MODES))
            outs.append(gain * x + tree_sum([weights[m] * states[m] for m in range(MODES)]))
        wide[pl.ds(at, 2 * SUB), :] = jnp.concatenate(outs, axis=0)
        return states

    zero = jnp.zeros((SUB, LANES), F32)
    lax.fori_loop(0, CHUNK // 2, tokens, (zero,) * MODES, unroll=4)
    for g in range(SUB):
        y_ref[:, g * LANES : (g + 1) * LANES] = wide[pl.ds(g, CHUNK, stride=SUB), :]


def final_kernel(start_ref, basis_ref, first_ref, second_ref, q_ref, out_ref):
    values = jnp.concatenate([start_ref[g ^ HALF_FLIP].astype(F32) for g in range(MANY)], axis=1)
    values = jnp.concatenate([values] * 3, axis=0).astype(BF16)
    carried = jnp.dot(basis_ref[...], values, preferred_element_type=F32)
    for half, own_ref in enumerate((first_ref, second_ref)):

        @pl.when(pl.program_id(0) == half)
        def _():
            pre = own_ref[...] + carried
            out_ref[...] = (q_ref[...].astype(F32) * pre.astype(BF16).astype(F32)).astype(BF16)


def local(queries, key_proj, value_proj, decay_rate, residue, skip_gain, *, interpret=False):
    tokens, channels = queries.shape
    groups = channels // LANES
    grid = channels // WIDE
    nseq = lax.axis_size("seq")
    nodes, basis = node_tables()

    def call(kernel, name, flops, nbytes, **kw):
        return pl.pallas_call(
            kernel,
            name=name,
            cost_estimate=pl.CostEstimate(flops=flops, bytes_accessed=nbytes, transcendentals=0),
            interpret=interpret,
            **kw,
        )

    def exchange(array, axis, root):
        order = [i ^ root for i in range(array.shape[0])]
        return lax.all_to_all(
            array, axis, split_axis=0, concat_axis=0, tiled=True, axis_index_groups=[order]
        )

    def in_hbm(array):
        return pltpu.with_memory_space_constraint(array, pltpu.HBM)

    struct = jax.ShapeDtypeStruct
    tight = pltpu.CompilerParams(vmem_limit_bytes=16 * 1024 * 1024)
    halves = pl.BlockSpec((CHUNK, MANY * LANES), lambda i: (0, i))
    anywhere = pl.BlockSpec(memory_space=pl.ANY)
    whole = pl.BlockSpec(memory_space=pltpu.VMEM)

    def fixed(*shape):
        return pl.BlockSpec(shape, lambda i: (0,) * len(shape))

    def stack(depth):
        return pl.BlockSpec((MANY, depth, LANES), lambda i: (i ^ (ROOT_CTX // MANY), 0, 0))

    sums = call(
        moments_kernel, "moments", 100_000_000, 3_000_000,
        grid=(2,),
        in_specs=[
            halves, halves, fixed(3 * SAMPLES, CHUNK),
            fixed(MODES, LANES), fixed(MODES, LANES), fixed(1, LANES),
        ],
        out_specs=stack(ROWS),
        out_shape=struct((groups, ROWS, LANES), BF16),
        scratch_shapes=[pltpu.VMEM((2 * MODES, LANES), F32)],
    )(key_proj, value_proj, jnp.asarray(basis), decay_rate, residue, skip_gain[None, :])
    got = exchange(sums, "ctx", ROOT_CTX)

    def mix(half):
        return call(
            mix_kernel, "mix", 1_000_000_000, 2_000_000,
            grid=(grid // 2,),
            in_specs=[pl.BlockSpec((CHUNK, WIDE), lambda i: (0, i + half * (grid // 2)))] * 2,
            out_specs=pl.BlockSpec((CHUNK * SUB, LANES), lambda i: (i, 0)),
            out_shape=struct((grid // 2 * CHUNK * SUB, LANES), BF16),
            scratch_shapes=[pltpu.VMEM((CHUNK * SUB, LANES), F32)],
            compiler_params=tight,
        )(in_hbm(key_proj), in_hbm(value_proj))

    mixed = [mix(0), mix(1)]

    before, end_state = call(
        lambda *refs: block_kernel(nodes, *refs), "block", 300_000, 500_000,
        grid=(1,),
        in_specs=[fixed(groups, SAMPLES, LANES), fixed(MODES, LANES), anywhere, anywhere],
        out_specs=[fixed(groups, MODES, LANES), fixed(nseq, MODES, LANES)],
        out_shape=[struct((groups, MODES, LANES), F32), struct((nseq, MODES, LANES), F32)],
        compiler_params=tight,
    )(got, decay_rate, *mixed)
    blocks = exchange(end_state, "seq", ROOT_SEQ)

    def respond(half, after):
        steps = grid // 2
        return call(
            inner_kernel, "inner", 1_000_000_000, 2_500_000,
            grid=(steps,),
            in_specs=[
                pl.BlockSpec((CHUNK * SUB, LANES), lambda i: (i, 0)),
                pl.BlockSpec((SUB, ROWS, LANES), lambda i: ((i + half * steps) ^ BLOCK_FLIP, 0, 0)),
                anywhere,
            ],
            out_specs=pl.BlockSpec((CHUNK, WIDE), lambda i: (0, i)),
            out_shape=struct((tokens, channels // 2), F32),
            scratch_shapes=[pltpu.VMEM((SUB * ROWS, LANES), F32), pltpu.VMEM((CHUNK * SUB, LANES), F32)],
            compiler_params=tight,
        )(mixed[half], got, after)

    first = respond(0, end_state)

    starts = call(
        lambda *refs: link_kernel(nodes, *refs), "link", 300_000, 500_000,
        in_specs=[pl.BlockSpec(memory_space=pltpu.SMEM)] + [pl.BlockSpec(memory_space=pltpu.VMEM)] * 4 + [anywhere],
        out_shape=struct((groups, SAMPLES, LANES), BF16),
        compiler_params=tight,
    )(
        lax.axis_index("seq").astype(jnp.int32)[None],
        before, blocks, decay_rate, residue, first,
    )
    second = respond(1, starts)
    starts = exchange(starts, "ctx", ROOT_CTX)

    return call(
        final_kernel, "final", 100_000_000, 5_000_000,
        grid=(2,),
        in_specs=[stack(SAMPLES), fixed(CHUNK, 3 * SAMPLES), whole, whole, halves],
        out_specs=halves,
        out_shape=struct((tokens, channels), BF16),
        compiler_params=tight,
    )(starts, jnp.asarray(basis.T), first, second, in_hbm(queries))


def solution(mesh):
    rows = P(("seq", "ctx"), None)
    return jax.shard_map(
        local,
        mesh=mesh,
        in_specs=(rows, rows, rows, P(None, "ctx"), P(None, "ctx"), P("ctx")),
        out_specs=rows,
        check_vma=False,
    )
```

```python
import jax
import jax.numpy as jnp
import ml_dtypes
import numpy as np
from jax import lax
from jax.experimental import pallas as pl
from jax.experimental.pallas import tpu as pltpu
from jax.sharding import PartitionSpec as P

F32, BF16 = jnp.float32, jnp.bfloat16
LANES = 128
SUB = 8
WIDE = SUB * LANES
MANY = 16
CHUNK = 128
MODES = 16
NODES = 23
SAMPLES = 24
ROWS = SAMPLES + 2 * MODES
GAIN = SAMPLES - 1
ROOT_CTX, ROOT_SEQ = 21, 4
BLOCK_FLIP, GROUP_FLIP, HALF_FLIP = ROOT_CTX // SUB, ROOT_CTX % SUB, ROOT_CTX % MANY


def node_tables():
    half = (CHUNK - 1) / 2.0
    nodes = half + half * np.cos((2.0 * np.arange(NODES) + 1.0) * np.pi / (2.0 * NODES))
    at = np.arange(CHUNK, dtype=np.float64)
    basis = np.zeros((SAMPLES, CHUNK))
    for k in range(NODES):
        others = np.delete(nodes, k)
        basis[k] = np.prod((at[:, None] - others) / (nodes[k] - others), axis=1)
    parts, left = [], basis
    for _ in range(3):
        part = left.astype(ml_dtypes.bfloat16)
        parts.append(part)
        left = left - part.astype(np.float64)
    return [float(n) for n in nodes], np.concatenate(parts)


def one_minus_exp(x):
    series = jnp.ones_like(x)
    for order in range(9, 1, -1):
        series = 1.0 - x * (1.0 / order) * series
    return jnp.where(x < 0.5, x * series, 1.0 - jnp.exp(-x))


def mode_weights(rate, resid):
    return resid * jnp.sqrt(one_minus_exp(2.0 * rate))


def product(k, v):
    return (k.astype(F32) * v.astype(F32)).astype(BF16)


def tree_sum(terms):
    while len(terms) > 1:
        pairs = [terms[i] + terms[i + 1] for i in range(0, len(terms) - 1, 2)]
        terms = pairs + terms[len(terms) - len(terms) % 2 :]
    return terms[0]


def moments_kernel(k_ref, v_ref, basis_ref, rate_ref, resid_ref, gain_ref, out_ref, par):
    @pl.when(pl.program_id(0) == 0)
    def _():
        rate = rate_ref[...]
        par[0:MODES, :] = rate
        par[MODES : 2 * MODES, :] = mode_weights(rate, resid_ref[...])

    sums = jnp.dot(basis_ref[...], product(k_ref[...], v_ref[...]), preferred_element_type=F32)
    sums = sums[0:SAMPLES] + sums[SAMPLES : 2 * SAMPLES] + sums[2 * SAMPLES :]
    spot = lax.broadcasted_iota(jnp.int32, (SAMPLES, LANES), 0) == GAIN
    gain = jnp.broadcast_to(gain_ref[...], (SAMPLES, LANES))
    for g in range(MANY):
        part = jnp.where(spot, gain, sums[:, g * LANES : (g + 1) * LANES])
        out_ref[g ^ HALF_FLIP] = jnp.concatenate([part, par[...]], axis=0).astype(BF16)


def mix_kernel(k_ref, v_ref, out_ref, wide):
    for g in range(SUB):
        cols = slice(g * LANES, (g + 1) * LANES)
        wide[pl.ds(g, CHUNK, stride=SUB), :] = product(k_ref[:, cols], v_ref[:, cols]).astype(F32)
    out_ref[...] = wide[...].astype(BF16)


def block_kernel(nodes, got_ref, rate_ref, after_ref, also_ref, before_ref, end_ref):
    rate = rate_ref[...]
    decay = jnp.exp(-float(CHUNK) * rate)
    reach = [jnp.exp(-(CHUNK - 1.0 - node) * rate) for node in nodes]
    state = jnp.zeros((MODES, LANES), F32)
    for d in range(before_ref.shape[0]):
        before_ref[d] = state
        sums = got_ref[d ^ ROOT_CTX, 0:SAMPLES, :].astype(F32)
        end = tree_sum(
            [reach[k] * jnp.broadcast_to(sums[k : k + 1, :], (MODES, LANES)) for k in range(NODES)]
        )
        state = decay * state + end
    for z in range(end_ref.shape[0]):
        end_ref[z] = state


def link_kernel(nodes, place_ref, before_ref, blocks_ref, rate_ref, resid_ref, after_ref, out_ref):
    nchunks = before_ref.shape[0]
    place = place_ref[0]
    rate = rate_ref[...]
    span = jnp.exp(-float(CHUNK * nchunks) * rate)
    start = jnp.zeros((MODES, LANES), F32)
    for z in range(blocks_ref.shape[0]):
        start = jnp.where(z < place, span * start + blocks_ref[z ^ ROOT_SEQ], start)
    decay = jnp.exp(-float(CHUNK) * rate)
    lift = mode_weights(rate, resid_ref[...]) * jnp.exp(-rate)
    spot = lax.broadcasted_iota(jnp.int32, (SAMPLES, LANES), 0)
    column = jnp.zeros((SAMPLES, LANES), F32)
    for k, node in enumerate(nodes):
        column = jnp.where(spot == k, node, column)
    reach = [
        jnp.exp(-column * jnp.broadcast_to(rate[m : m + 1, :], (SAMPLES, LANES))) for m in range(MODES)
    ]
    for d in range(nchunks):
        lifted = lift * (before_ref[d] + start)
        out_ref[d ^ ROOT_CTX] = tree_sum(
            [reach[m] * jnp.broadcast_to(lifted[m : m + 1, :], (SAMPLES, LANES)) for m in range(MODES)]
        ).astype(BF16)
        start = decay * start


def inner_kernel(x_ref, got_ref, after_ref, y_ref, rows, wide):
    for g in range(SUB):
        rows[g * ROWS : (g + 1) * ROWS, :] = got_ref[g ^ GROUP_FLIP].astype(F32)

    def row(place):
        return rows[pl.ds(place, SUB, stride=ROWS), :]

    powers = [jnp.exp(-row(SAMPLES + m)) for m in range(MODES)]
    weights = [row(SAMPLES + MODES + m) for m in range(MODES)]
    gain = row(GAIN)

    def tokens(t, states):
        at = pl.multiple_of(t * 2 * SUB, 2 * SUB)
        pair = x_ref[pl.ds(at, 2 * SUB), :].astype(F32)
        outs = []
        for x in (pair[:SUB], pair[SUB:]):
            states = tuple(powers[m] * states[m] + x for m in range(MODES))
            outs.append(gain * x + tree_sum([weights[m] * states[m] for m in range(MODES)]))
        wide[pl.ds(at, 2 * SUB), :] = jnp.concatenate(outs, axis=0)
        return states

    zero = jnp.zeros((SUB, LANES), F32)
    lax.fori_loop(0, CHUNK // 2, tokens, (zero,) * MODES, unroll=4)
    for g in range(SUB):
        y_ref[:, g * LANES : (g + 1) * LANES] = wide[pl.ds(g, CHUNK, stride=SUB), :]


def final_kernel(start_ref, basis_ref, first_ref, second_ref, q_ref, out_ref):
    values = jnp.concatenate([start_ref[g ^ HALF_FLIP].astype(F32) for g in range(MANY)], axis=1)
    values = jnp.concatenate([values] * 3, axis=0).astype(BF16)
    carried = jnp.dot(basis_ref[...], values, preferred_element_type=F32)
    for half, own_ref in enumerate((first_ref, second_ref)):

        @pl.when(pl.program_id(0) == half)
        def _():
            pre = own_ref[...] + carried
            out_ref[...] = (q_ref[...].astype(F32) * pre.astype(BF16).astype(F32)).astype(BF16)


def local(queries, key_proj, value_proj, decay_rate, residue, skip_gain, *, interpret=False):
    tokens, channels = queries.shape
    groups = channels // LANES
    grid = channels // WIDE
    nseq = lax.axis_size("seq")
    nodes, basis = node_tables()

    def call(kernel, name, flops, nbytes, **kw):
        return pl.pallas_call(
            kernel,
            name=name,
            cost_estimate=pl.CostEstimate(flops=flops, bytes_accessed=nbytes, transcendentals=0),
            interpret=interpret,
            **kw,
        )

    def exchange(array, axis, root):
        order = [i ^ root for i in range(array.shape[0])]
        return lax.all_to_all(
            array, axis, split_axis=0, concat_axis=0, tiled=True, axis_index_groups=[order]
        )

    def in_hbm(array):
        return pltpu.with_memory_space_constraint(array, pltpu.HBM)

    struct = jax.ShapeDtypeStruct
    tight = pltpu.CompilerParams(vmem_limit_bytes=16 * 1024 * 1024)
    halves = pl.BlockSpec((CHUNK, MANY * LANES), lambda i: (0, i))
    anywhere = pl.BlockSpec(memory_space=pl.ANY)
    whole = pl.BlockSpec(memory_space=pltpu.VMEM)

    def fixed(*shape):
        return pl.BlockSpec(shape, lambda i: (0,) * len(shape))

    def stack(depth):
        return pl.BlockSpec((MANY, depth, LANES), lambda i: (i ^ (ROOT_CTX // MANY), 0, 0))

    sums = call(
        moments_kernel, "moments", 100_000_000, 3_000_000,
        grid=(2,),
        in_specs=[
            halves, halves, fixed(3 * SAMPLES, CHUNK),
            fixed(MODES, LANES), fixed(MODES, LANES), fixed(1, LANES),
        ],
        out_specs=stack(ROWS),
        out_shape=struct((groups, ROWS, LANES), BF16),
        scratch_shapes=[pltpu.VMEM((2 * MODES, LANES), F32)],
    )(key_proj, value_proj, jnp.asarray(basis), decay_rate, residue, skip_gain[None, :])
    got = exchange(sums, "ctx", ROOT_CTX)

    def mix(half):
        return call(
            mix_kernel, "mix", 1_000_000_000, 2_000_000,
            grid=(grid // 2,),
            in_specs=[pl.BlockSpec((CHUNK, WIDE), lambda i: (0, i + half * (grid // 2)))] * 2,
            out_specs=pl.BlockSpec((CHUNK * SUB, LANES), lambda i: (i, 0)),
            out_shape=struct((grid // 2 * CHUNK * SUB, LANES), BF16),
            scratch_shapes=[pltpu.VMEM((CHUNK * SUB, LANES), F32)],
            compiler_params=tight,
        )(in_hbm(key_proj), in_hbm(value_proj))

    mixed = [mix(0), mix(1)]

    before, end_state = call(
        lambda *refs: block_kernel(nodes, *refs), "block", 300_000, 500_000,
        grid=(1,),
        in_specs=[whole, fixed(MODES, LANES), anywhere, anywhere],
        out_specs=[fixed(groups, MODES, LANES), fixed(nseq, MODES, LANES)],
        out_shape=[struct((groups, MODES, LANES), F32), struct((nseq, MODES, LANES), F32)],
        compiler_params=tight,
    )(got, decay_rate, *mixed)
    blocks = exchange(end_state, "seq", ROOT_SEQ)

    def respond(half, after):
        steps = grid // 2
        return call(
            inner_kernel, "inner", 1_000_000_000, 2_500_000,
            grid=(steps,),
            in_specs=[
                pl.BlockSpec((CHUNK * SUB, LANES), lambda i: (i, 0)),
                pl.BlockSpec((SUB, ROWS, LANES), lambda i: ((i + half * steps) ^ BLOCK_FLIP, 0, 0)),
                anywhere,
            ],
            out_specs=pl.BlockSpec((CHUNK, WIDE), lambda i: (0, i)),
            out_shape=struct((tokens, channels // 2), F32),
            scratch_shapes=[pltpu.VMEM((SUB * ROWS, LANES), F32), pltpu.VMEM((CHUNK * SUB, LANES), F32)],
            compiler_params=tight,
        )(mixed[half], got, after)

    first = respond(0, end_state)

    starts = call(
        lambda *refs: link_kernel(nodes, *refs), "link", 300_000, 500_000,
        in_specs=[pl.BlockSpec(memory_space=pltpu.SMEM)] + [pl.BlockSpec(memory_space=pltpu.VMEM)] * 4 + [anywhere],
        out_shape=struct((groups, SAMPLES, LANES), BF16),
        compiler_params=tight,
    )(
        lax.axis_index("seq").astype(jnp.int32)[None],
        before, blocks, decay_rate, residue, first,
    )
    second = respond(1, starts)
    starts = exchange(starts, "ctx", ROOT_CTX)

    return call(
        final_kernel, "final", 100_000_000, 5_000_000,
        grid=(2,),
        in_specs=[stack(SAMPLES), fixed(CHUNK, 3 * SAMPLES), whole, whole, halves],
        out_specs=halves,
        out_shape=struct((tokens, channels), BF16),
        compiler_params=tight,
    )(starts, jnp.asarray(basis.T), first, second, in_hbm(queries))


def solution(mesh):
    rows = P(("seq", "ctx"), None)
    return jax.shard_map(
        local,
        mesh=mesh,
        in_specs=(rows, rows, rows, P(None, "ctx"), P(None, "ctx"), P("ctx")),
        out_specs=rows,
        check_vma=False,
    )
```
